256 devices in a mesh: atoms: 4 (over y), frames: 64 (over x, z, core).
Axes of the slice: x: 4, y: 4, z: 8, core: 2. Of those that a mesh axis runs over, the one named last changes fastest.
Arguments:
- frames: float32 [1536, 3, 98304], P('frames', None, 'atoms'), may hold values from -48 to 48
- mean_structure: float32 [3, 98304], P(None, 'atoms'), may hold values from -16 to 16
- atom_weight: float32 [98304], P('atoms'), may hold values from 1 to 32
- subspace: bfloat16 [32, 3, 98304], P(None, None, 'atoms'), may hold values from -6 to 6
Outputs:
- new_mean: float32 [3, 98304], P(None, ('atoms', 'frames'))
- image: float32 [32, 3, 98304], P(None, None, ('atoms', 'frames'))
- basis: float32 [32, 3, 98304], P(None, None, ('atoms', 'frames'))
The draws below stay inside these ranges and needn't reach their ends.
All inputs are finite; a program needn't handle non-finite values.
Results may differ from the reference program's by a relative error of at most 0.0076.
Values may be sent and summed in bfloat16 or wider, within the bound.
A program may use at most 128 MiB of HBM per device.

```python
import math
import jax
import jax.numpy as jnp
from jax import lax

A = 98304
K = 32
NEWTON = 8
F_DEV = 24
F = 1536


def structure_parts(key):
    index = jnp.arange(A).astype(jnp.float32)
    spread = 1.0 + 2.0 * index / (A - 1)
    plane = jax.random.truncated_normal(jax.random.fold_in(key, 11), -4.0, 4.0, (2, A), jnp.float32) * spread[None, :]
    depth = jax.random.truncated_normal(jax.random.fold_in(key, 12), -4.0, 4.0, (1, A), jnp.float32) * 0.5
    offset = jnp.array([1.0, -0.5, 0.3], jnp.float32)[:, None]
    return jnp.concatenate([plane, depth], axis=0) + offset


def collective_motion(key):
    pattern = jax.random.truncated_normal(jax.random.fold_in(key, 21), -4.0, 4.0, (4, 3, A), jnp.float32) * 0.5
    amplitude = jax.random.truncated_normal(jax.random.fold_in(key, 22), -4.0, 4.0, (F, 4), jnp.float32) * 0.15
    motion = amplitude[:, 0][:, None, None] * pattern[0][None]
    for mode in range(1, 4):
        motion = motion + amplitude[:, mode][:, None, None] * pattern[mode][None]
    return motion


def draw_mean_structure(key, part):
    return structure_parts(key)


def draw_frames(key, part):
    base = structure_parts(key)
    drift = jax.random.truncated_normal(jax.random.fold_in(key, 13), -4.0, 4.0, (3, A), jnp.float32) * 0.3
    noise = jax.random.truncated_normal(jax.random.fold_in(key, 14), -4.0, 4.0, (F, 3, A), jnp.float32) * 0.5
    angles = jax.random.uniform(jax.random.fold_in(key, 15), (3, F), jnp.float32, -math.pi, math.pi)
    shift = jax.random.truncated_normal(jax.random.fold_in(key, 16), -4.0, 4.0, (3, F), jnp.float32) * 2.0
    cosa, sina = (jnp.cos(angles[0]), jnp.sin(angles[0]))
    cosb, sinb = (jnp.cos(angles[1]), jnp.sin(angles[1]))
    cosc, sinc = (jnp.cos(angles[2]), jnp.sin(angles[2]))
    rows = [[cosa * cosb, cosa * sinb * sinc - sina * cosc, cosa * sinb * cosc + sina * sinc], [sina * cosb, sina * sinb * sinc + cosa * cosc, sina * sinb * cosc - cosa * sinc], [-sinb, cosb * sinc, cosb * cosc]]
    points = base[None] + drift[None] + noise + collective_motion(key)
    result = []
    for i in range(3):
        value = rows[i][0][:, None] * points[:, 0] + rows[i][1][:, None] * points[:, 1] + rows[i][2][:, None] * points[:, 2]
        result.append(value + shift[i][:, None])
    return jnp.stack(result, axis=1)


def block_scale(stream_key, extent, pieces, low, top_value):
    factor_of, own = 1.0, jax.random.fold_in(stream_key, 6)
    for position, shards_of in pieces:
        draws = jnp.exp(jax.random.uniform(jax.random.fold_in(own, position), (shards_of,), jnp.float32, low / len(pieces), top_value / len(pieces)))
        factor_of = factor_of * jnp.repeat(draws, extent[position] // shards_of).reshape([-1 if axis == position else 1 for axis in range(len(extent))])
    return factor_of


def normal_values(own_key, dims, scale, bound, shards=(), kind=jnp.bfloat16):
    gain = block_scale(own_key, dims, shards, -0.22, 0.18) if shards else 1.0
    values = jax.random.normal(own_key, dims, jnp.float32) * scale * gain
    return jnp.minimum(jnp.maximum(values, -bound), bound).astype(kind)


def setup_inputs(seed: int = 0) -> dict:
    streams_of = jax.random.split(jax.random.key(seed), 5)
    frames = draw_frames(jax.random.fold_in(streams_of[4], 71), 0)
    mean_structure = draw_mean_structure(jax.random.fold_in(streams_of[4], 71), 0)
    atom_weight = jnp.clip(jnp.exp(math.log(32.0) - 3.465736 * jax.random.uniform(streams_of[2], (A,), jnp.float32) ** block_scale(streams_of[2], (A,), ((0, 4),), -0.2, 0.2)), 1.0, 32.0)
    subspace = normal_values(streams_of[3], (K, 3, A), 1.0, 6.0, ((2, 4),))
    return {"frames": frames, "mean_structure": mean_structure, "atom_weight": atom_weight, "subspace": subspace}


def newton_polar(moment):
    norm = jnp.sqrt(lax.optimization_barrier(jnp.sum(moment * moment, axis=(1, 2))))
    x = moment / norm[:, None, None]
    for step in range(NEWTON):
        x00, x01, x02 = (x[:, 0, 0], x[:, 0, 1], x[:, 0, 2])
        x10, x11, x12 = (x[:, 1, 0], x[:, 1, 1], x[:, 1, 2])
        x20, x21, x22 = (x[:, 2, 0], x[:, 2, 1], x[:, 2, 2])
        c00 = x11 * x22 - x12 * x21
        c01 = x12 * x20 - x10 * x22
        c02 = x10 * x21 - x11 * x20
        c10 = x02 * x21 - x01 * x22
        c11 = x00 * x22 - x02 * x20
        c12 = x01 * x20 - x00 * x21
        c20 = x01 * x12 - x02 * x11
        c21 = x02 * x10 - x00 * x12
        c22 = x00 * x11 - x01 * x10
        determ = x00 * c00 + x01 * c01 + x02 * c02
        cofac = jnp.stack([jnp.stack([c00, c01, c02], axis=1), jnp.stack([c10, c11, c12], axis=1), jnp.stack([c20, c21, c22], axis=1)], axis=1)
        x = 0.5 * (x + cofac / determ[:, None, None])
    return x

def reference(frames, mean_structure, atom_weight, subspace):
    highest = lax.Precision.HIGHEST
    total = jnp.sum(atom_weight)
    mean_center = lax.optimization_barrier(jnp.sum(atom_weight[None, :] * mean_structure, axis=1)) / total
    frame_center = jnp.einsum('a,fia->fi', atom_weight, frames, precision=highest) / total
    centered = (mean_structure - mean_center[:, None]) * atom_weight[None, :]
    moment = jnp.einsum('ia,fja->fij', centered, frames, precision=highest) / total
    rotation = newton_polar(moment)
    anchor = mean_center[:, None] - mean_structure

    def align_block(inputs):
        block, rot, center = inputs
        moved = jnp.einsum('fij,fja->fia', rot, block, precision=highest)
        offset = jnp.einsum('fij,fj->fi', rot, center, precision=highest)
        return (moved - offset[:, :, None] + anchor[None]).astype(jnp.bfloat16)
    blocks = F // F_DEV
    displaced = lax.map(align_block, (frames.reshape(blocks, F_DEV, 3, A), rotation.reshape(blocks, F_DEV, 3, 3), frame_center.reshape(blocks, F_DEV, 3)))
    displaced = displaced.reshape(F, 3 * A)
    new_mean = mean_structure + lax.optimization_barrier(jnp.sum(displaced, axis=0, dtype=jnp.float32)).reshape(3, A) / F
    projection = jnp.dot(displaced.astype(jnp.float32), subspace.reshape(K, 3 * A).T.astype(jnp.float32), preferred_element_type=jnp.float32)
    centered_projection = (projection - lax.optimization_barrier(jnp.sum(projection, axis=0)) / F).astype(jnp.bfloat16)
    flat = jnp.dot(centered_projection.T.astype(jnp.float32), displaced.astype(jnp.float32), preferred_element_type=jnp.float32) / F
    gram = jnp.dot(flat, flat.T, precision=highest) / (3 * A)
    lower = jnp.linalg.cholesky(gram)
    basis = jax.scipy.linalg.solve_triangular(lower, flat, lower=True)
    return (new_mean, flat.reshape(K, 3, A), basis.reshape(K, 3, A))
```

```python
import jax
import jax.numpy as jnp
from jax import lax
from jax.experimental import pallas as pl
from jax.experimental.pallas import tpu as pltpu
from jax.sharding import PartitionSpec as P

ATOMS = 98304
FRAMES = 1536
NEWTON = 8
NX, NZ, NC, NY = 4, 8, 2, 4
NF = 24
FP = 32
K = 32
AL = ATOMS // NY
BLK = AL // (NX * NZ * NC)
NB = NX * NZ
CHUNKS = 8
CW = AL // CHUNKS
STEP = 512
F32 = jnp.float32
BF16 = jnp.bfloat16
MESH = pl.DeviceIdType.MESH
HIGHEST = lax.Precision.HIGHEST
STREAMS = tuple((h, d) for h in (0, 1) for d in (1, -1))
NT = (((1,), (1,)), ((), ()))


def steps_of(n, half, direction):
    return n // 2 if (direction == 1) == (half == 0) else n // 2 - 1


def newton(m):
    norm = m[0] * m[0]
    for e in m[1:]:
        norm = norm + e * e
    inv = 1.0 / jnp.sqrt(norm)
    x = [e * inv for e in m]
    for _ in range(NEWTON):
        x00, x01, x02, x10, x11, x12, x20, x21, x22 = x
        cof = [
            x11 * x22 - x12 * x21,
            x12 * x20 - x10 * x22,
            x10 * x21 - x11 * x20,
            x02 * x21 - x01 * x22,
            x00 * x22 - x02 * x20,
            x01 * x20 - x00 * x21,
            x01 * x12 - x02 * x11,
            x02 * x10 - x00 * x12,
            x00 * x11 - x01 * x10,
        ]
        det = x00 * cof[0] + x01 * cof[1] + x02 * cof[2]
        r = 1.0 / det
        x = [0.5 * (a + c * r) for a, c in zip(x, cof)]
    return x


def kernel(
    x_hbm, ms_ref, w_ref, s_hbm, nm_ref, img_ref, bas_ref,
    xv, sv, dall, dsend, rot, ex1, ex2, pp, gsq, pbx, pbz, cpt, gx, gy, gz,
    a1s, a1r, b1s, b1r, a2s, a2r, b2s, b2r, acca, accb,
    xsem, ssem, y1s, y1r, y2s, y2r, px_s, px_r, pz_s, pz_r, pp_s, pp_r, dx_s, dx_r,
    gx_s, gx_r, gy_s, gy_r, gz_s, gz_r, a1ss, a1rs, b1ss, b1rs, a2ss, a2rs, b2ss, b2rs,
):
    y = lax.axis_index("atoms")
    n = lax.axis_index("frames")
    px = n // (NZ * NC)
    pz = (n // NC) % NZ
    pc = n % NC

    def dev(dx=0, dz=0, dc=0, dy=0):
        tx = (px + (dx + NX)) % NX
        tz = (pz + (dz + NZ)) % NZ
        tc = (pc + dc) % NC
        return ((y + dy) % NY, (tx * NZ + tz) * NC + tc)

    y_peers = [dev(dy=j) for j in range(1, NY)]
    xc_peers = [dev(dx=j // 2, dc=j % 2) for j in range(1, NX * NC)]
    z_peers = [dev(dz=j) for j in range(1, NZ)]
    partner = dev(dc=1)

    loads = []
    for q in range(CHUNKS):
        cols = pl.ds(q * CW, CW)
        cp = pltpu.make_async_copy(x_hbm.at[:, :, cols], xv.at[:, :, cols], xsem.at[q])
        cp.start()
        loads.append(cp)
    sload = pltpu.make_async_copy(s_hbm, sv, ssem)
    sload.start()

    barrier = pltpu.get_barrier_semaphore()
    for peer in y_peers + xc_peers + z_peers:
        pl.semaphore_signal(barrier, inc=1, device_id=peer, device_id_type=MESH)

    def remote(src, dst, ssm, rsm, peer):
        return pltpu.make_async_remote_copy(
            src_ref=src, dst_ref=dst, send_sem=ssm, recv_sem=rsm, device_id=peer, device_id_type=MESH
        )

    pending = []

    def exchange(buf, peers, ssm, rsm):
        copies = []
        for j, peer in enumerate(peers):
            copies.append(remote(buf.at[0], buf.at[j + 1], ssm.at[j], rsm.at[j], peer))
        for c in copies:
            c.start()
        for c in copies:
            c.wait_recv()
        pending.extend(copies)

    lane = lax.broadcasted_iota(jnp.int32, (NF, 128), 1)

    def center_body(q, carry):
        tw, tm = carry
        cols = pl.ds(pl.multiple_of(q * 2048, 2048), 2048)
        wv = w_ref[:, cols]
        return tw + wv, tm + ms_ref[:, cols] * wv

    tw, tm = lax.fori_loop(
        0, AL // 2048, center_body, (jnp.zeros((1, 2048), F32), jnp.zeros((3, 2048), F32))
    )
    tw = jnp.sum(tw, axis=1, keepdims=True)
    tm = jnp.sum(tm, axis=1, keepdims=True)
    lc = tm / tw

    def sums_body(q, acc):
        acc = list(acc)
        cols = pl.ds(pl.multiple_of(q * STEP, STEP), STEP)
        wv = w_ref[:, cols]
        wm = (ms_ref[:, cols] - lc) * wv
        for t in range(STEP // 128):
            lo = t * 128
            sub = pl.ds(pl.multiple_of(q * STEP + lo, 128), 128)
            wt = jnp.broadcast_to(wv[:, lo : lo + 128], (NF, 128))
            mt = [jnp.broadcast_to(wm[i : i + 1, lo : lo + 128], (NF, 128)) for i in range(3)]
            for j in range(3):
                xj = xv[j, :, sub]
                acc[j] = acc[j] + xj * wt
                for i in range(3):
                    acc[3 + i * 3 + j] = acc[3 + i * 3 + j] + xj * mt[i]
        return tuple(acc)

    acc = tuple(jnp.zeros((NF, 128), F32) for _ in range(12))
    per = CW // STEP
    for q in range(CHUNKS):
        loads[q].wait()
        acc = lax.fori_loop(q * per, (q + 1) * per, sums_body, acc)
    cols16 = [jnp.broadcast_to(tw, (NF, 1))] + [jnp.broadcast_to(tm[i : i + 1], (NF, 1)) for i in range(3)]
    cols16 += [jnp.sum(a, axis=1, keepdims=True) for a in acc]
    tile = jnp.zeros((NF, 128), F32)
    for q, col in enumerate(cols16):
        tile = jnp.where(lane == q, jnp.broadcast_to(col, (NF, 128)), tile)
    ex1[0] = tile
    pl.semaphore_wait(barrier, len(y_peers) + len(xc_peers) + len(z_peers))
    exchange(ex1, y_peers, y1s, y1r)

    slots = [ex1[j] for j in range(NY)]
    part = [[s[:, q : q + 1] for q in range(16)] for s in slots]
    total = part[0][0] + part[1][0] + part[2][0] + part[3][0]
    mc = [(part[0][1 + i] + part[1][1 + i] + part[2][1 + i] + part[3][1 + i]) / total for i in range(3)]
    fc = [(part[0][4 + j] + part[1][4 + j] + part[2][4 + j] + part[3][4 + j]) / total for j in range(3)]
    moment = []
    shift_c = [[p[1 + i] / p[0] - mc[i] for i in range(3)] for p in part]
    for i in range(3):
        for j in range(3):
            m = None
            for p, sc in zip(part, shift_c):
                term = p[7 + i * 3 + j] + sc[i] * p[4 + j]
                m = term if m is None else m + term
            moment.append(m / total)
    r = newton(moment)
    for q in range(9):
        rot[q] = jnp.broadcast_to(r[q], (NF, 128))
    for i in range(3):
        off = r[3 * i] * fc[0] + r[3 * i + 1] * fc[1] + r[3 * i + 2] * fc[2]
        rot[9 + i] = jnp.broadcast_to(mc[i] - off, (NF, 128))

    sload.wait()

    def move_body(own):
        def body(b, acc):
            core = pc if own else 1 - pc
            base = (b * NC + core) * BLK
            for i in range(3):
                pieces = []
                for t in range(BLK // 128):
                    sub = pl.ds(pl.multiple_of(base + t * 128, 128), 128)
                    v = rot[3 * i] * xv[0, :, sub] + rot[3 * i + 1] * xv[1, :, sub] + rot[3 * i + 2] * xv[2, :, sub]
                    v = v + rot[9 + i] - jnp.broadcast_to(ms_ref[i : i + 1, sub], (NF, 128))
                    pieces.append(v)
                v = jnp.concatenate(pieces, axis=1)
                v = jnp.concatenate([v, jnp.zeros((FP - NF, BLK), F32)], axis=0).astype(BF16)
                if own:
                    dall[b, i, 0:FP, :] = v
                else:
                    dsend[b, i] = v
                cols = pl.ds(pl.multiple_of(base, 128), BLK)
                acc = acc + lax.dot_general(sv[i, :, cols], v, NT, preferred_element_type=F32)
            return acc

        return body

    pacc = lax.fori_loop(0, NB, move_body(False), jnp.zeros((K, FP), F32))
    dcopy = remote(dsend, dall.at[:, :, FP : 2 * FP, :], dx_s, dx_r, partner)
    dcopy.start()
    pacc = lax.fori_loop(0, NB, move_body(True), pacc)

    ex2[0] = jnp.zeros((K, 128), F32)
    ex2[0, :, 0:FP] = pacc
    exchange(ex2, y_peers, y2s, y2r)
    ptot = ex2[0] + ex2[1] + ex2[2] + ex2[3]
    pp[0] = ptot
    pcopy = remote(pp.at[0], pp.at[1], pp_s, pp_r, partner)
    pcopy.start()
    rows = lax.broadcasted_iota(jnp.int32, (K, 128), 0)
    lanes = lax.broadcasted_iota(jnp.int32, (K, 128), 1)
    col = jnp.broadcast_to(jnp.sum(ptot, axis=1, keepdims=True), (K, 128))
    row = jnp.sum(jnp.where(rows == lanes, col, 0.0), axis=0, keepdims=True)
    pbx[0] = jnp.broadcast_to(row, (8, 128))
    exchange(pbx, xc_peers, px_s, px_r)
    v = pbx[0]
    for j in range(1, NX * NC):
        v = v + pbx[j]
    pbz[0] = v
    exchange(pbz, z_peers, pz_s, pz_r)
    v = pbz[0]
    for j in range(1, NZ):
        v = v + pbz[j]
    row = jnp.broadcast_to(v[0:1], (K, 128))
    pbar = jnp.sum(jnp.where(rows == lanes, row, 0.0), axis=1, keepdims=True) / FRAMES
    pcopy.wait_recv()
    other = pltpu.roll(pp[1], FP, 1)
    both = jnp.where(lanes < FP, ptot, other) - pbar
    cpt[...] = both.astype(BF16)
    dcopy.wait_recv()

    erow = lax.broadcasted_iota(jnp.int32, (16, 2 * FP), 0)
    ones = [jnp.where(erow == i, 1.0, 0.0).astype(BF16) for i in range(3)]

    def mm(lhs, rhs):
        return jnp.dot(lhs, rhs, preferred_element_type=F32)

    def term_a(dest, h, emit):
        def body(q, c):
            blk = dest * NZ + h * (NZ // 2) + q
            for i in range(2):
                emit(q, i, mm(cpt[:, 0 : 2 * FP], dall[blk, i]))
            return c

        lax.fori_loop(0, NZ // 2, body, 0)

    def term_b(dest, h, emit):
        def body(q, c):
            blk = (h * (NX // 2) + q) * NZ + dest
            emit(q, 0, mm(cpt[:, 0 : 2 * FP], dall[blk, 2]))
            sh = mm(ones[0], dall[blk, 0]) + mm(ones[1], dall[blk, 1]) + mm(ones[2], dall[blk, 2])
            emit(q, 1, sh)
            return c

        lax.fori_loop(0, NX // 2, body, 0)

    def rowslice(i):
        return slice(32 * i, 32 * i + 32)

    def brow(i):
        return slice(0, 32) if i == 0 else slice(32, 48)

    class Stage:
        def __init__(self, length, pos, sbuf, rbuf, ssm, rsm, fill, peer_of, cut):
            self.length, self.pos, self.sbuf, self.rbuf = length, pos, sbuf, rbuf
            self.ssm, self.rsm, self.fill, self.peer_of, self.cut = ssm, rsm, fill, peer_of, cut
            self.copies = {}

        def send(self, st, s):
            h, d = STREAMS[st]
            total_steps = steps_of(self.length, h, d)
            if s >= total_steps:
                return
            dest = (self.pos + (d * (total_steps - s) + self.length)) % self.length
            if s == 0:
                src = self.sbuf.at[st]
                self.fill(src, dest, h, False)
            else:
                self.copies[st, s - 1].wait_recv()
                src = self.rbuf.at[st, s - 1]
                self.fill(src, dest, h, True)
            c = remote(
                self.cut(src, h), self.cut(self.rbuf.at[st, s], h), self.ssm.at[st, s], self.rsm.at[st, s],
                self.peer_of(d),
            )
            c.start()
            pending.append(c)
            self.copies[st, s] = c

        def finals(self, h):
            out = []
            for st, (hh, d) in enumerate(STREAMS):
                if hh == h:
                    s = steps_of(self.length, h, d) - 1
                    self.copies[st, s].wait_recv()
                    out.append(self.rbuf.at[st, s])
            return out

    def fill_a1(ref, dest, h, add):
        def emit(q, i, t):
            if add:
                t = t + ref[q, rowslice(i), :].astype(F32)
            ref[q, rowslice(i), :] = t.astype(BF16)

        term_a(dest, h, emit)

    def fill_b1(ref, dest, h, add):
        def emit(q, i, t):
            if add:
                t = t + ref[q, brow(i), :].astype(F32)
            ref[q, brow(i), :] = t.astype(BF16)

        term_b(dest, h, emit)

    def fill_a2(ref, dest, h, add):
        t = acca[dest, rowslice(h), :]
        if add:
            t = t + ref[...].astype(F32)
        ref[...] = t.astype(BF16)

    def fill_b2(ref, dest, h, add):
        if h == 0:
            t = accb[dest, 0:32, :]
            if add:
                t = t + ref[...].astype(F32)
            ref[...] = t.astype(BF16)
        else:
            t = accb[dest, 32:48, :]
            if add:
                t = t + ref[0:16, :].astype(F32)
            ref[0:16, :] = t.astype(BF16)

    def whole(ref, h):
        return ref

    def cut_b2(ref, h):
        return ref if h == 0 else ref.at[0:16, :]

    x_dir = {1: dev(dx=1), -1: dev(dx=-1)}
    z_dir = {1: dev(dz=1), -1: dev(dz=-1)}
    sa1 = Stage(NX, px, a1s, a1r, a1ss, a1rs, fill_a1, x_dir.get, whole)
    sb1 = Stage(NZ, pz, b1s, b1r, b1ss, b1rs, fill_b1, z_dir.get, whole)
    sa2 = Stage(NZ, pz, a2s, a2r, a2ss, a2rs, fill_a2, z_dir.get, whole)
    sb2 = Stage(NX, px, b2s, b2r, b2ss, b2rs, fill_b2, x_dir.get, cut_b2)

    order = (0, 3, 2, 1)
    for st in order:
        sa1.send(st, 0)
        sb1.send(st, 0)
    for st in order:
        sb1.send(st, 1)
    for st in order:
        sa1.send(st, 1)
    for st in order:
        sb1.send(st, 2)
    for st in order:
        sb1.send(st, 3)

    for h in (0, 1):
        f0, f1 = sa1.finals(h)

        def emit(q, i, t, f0=f0, f1=f1, h=h):
            t = t + f0[q, rowslice(i), :].astype(F32) + f1[q, rowslice(i), :].astype(F32)
            acca[h * (NZ // 2) + q, rowslice(i), :] = t

        term_a(px, h, emit)
    for st in order:
        sa2.send(st, 0)
    for h in (0, 1):
        f0, f1 = sb1.finals(h)

        def emit(q, i, t, f0=f0, f1=f1, h=h):
            t = t + f0[q, brow(i), :].astype(F32) + f1[q, brow(i), :].astype(F32)
            accb[h * (NX // 2) + q, brow(i), :] = t

        term_b(pz, h, emit)
    for st in order:
        sb2.send(st, 0)
    for st in order:
        sa2.send(st, 1)
    for st in order:
        sb2.send(st, 1)
    for st in order:
        sa2.send(st, 2)
    for st in order:
        sa2.send(st, 3)

    inv_f = 1.0 / FRAMES
    f0, f1 = sb2.finals(0)
    img2 = (accb[px, 0:32, :] + f0[...].astype(F32) + f1[...].astype(F32)) * inv_f
    f0, f1 = sb2.finals(1)
    shift = accb[px, 32:48, :] + f0[0:16, :].astype(F32) + f1[0:16, :].astype(F32)
    own = pl.ds(pl.multiple_of(n * BLK, 128), BLK)
    nm_ref[...] = ms_ref[:, own] + shift[0:3] * inv_f
    imgs = []
    for h in (0, 1):
        f0, f1 = sa2.finals(h)
        imgs.append((acca[pz, rowslice(h), :] + f0[...].astype(F32) + f1[...].astype(F32)) * inv_f)
    imgs.append(img2)
    g = None
    for i in range(3):
        img_ref[i] = imgs[i]
        t = lax.dot_general(imgs[i], imgs[i], NT, preferred_element_type=F32, precision=HIGHEST)
        g = t if g is None else g + t
    gsq[...] = jnp.zeros((K, 128), F32)
    gsq[:, 0:K] = g
    v = gsq[0:8, :]
    for q in range(1, 4):
        v = v + pltpu.roll(gsq[8 * q : 8 * q + 8, :], 32 * q, 1)
    gx[0] = v
    exchange(gx, xc_peers, gx_s, gx_r)
    v = gx[0]
    for j in range(1, NX * NC):
        v = v + gx[j]
    gy[0] = v
    exchange(gy, y_peers, gy_s, gy_r)
    gz[0] = gy[0] + gy[1] + gy[2] + gy[3]
    exchange(gz, z_peers, gz_s, gz_r)
    v = gz[0]
    for j in range(1, NZ):
        v = v + gz[j]
    v = v / (3 * ATOMS)
    m = jnp.concatenate([v] + [pltpu.roll(v, 128 - 32 * q, 1) for q in range(1, 4)], axis=0)
    m = jnp.where(lanes < K, m, jnp.where(lanes - K == rows, 1.0, 0.0))
    for j in range(K - 1):
        prow = jnp.broadcast_to(m[j : j + 1, :], (K, 128))
        pcol = jnp.broadcast_to(m[:, j : j + 1], (K, 128))
        piv = 1.0 / pcol[j : j + 1, :]
        m = jnp.where(rows > j, m - pcol * (prow * piv), m)
    diag = jnp.sum(jnp.where(rows == lanes, m, 0.0), axis=1, keepdims=True)
    linv = pltpu.roll(m, 128 - K, 1) * (1.0 / jnp.sqrt(diag))
    linv = linv[:, 0:K]
    for i in range(3):
        bas_ref[i] = jnp.dot(linv, imgs[i], preferred_element_type=F32, precision=HIGHEST)

    for c in pending + [dcopy, pcopy]:
        c.wait_send()


def per_device(frames, mean_structure, atom_weight, subspace):
    x = jnp.transpose(frames, (1, 0, 2))
    s = jnp.transpose(subspace, (1, 0, 2))
    vm = pl.BlockSpec(memory_space=pltpu.VMEM)
    anyspec = pl.BlockSpec(memory_space=pl.ANY)
    dma = pltpu.SemaphoreType.DMA
    V = pltpu.VMEM
    scratch = [
        V((3, NF, AL), F32), V((3, K, AL), BF16), V((NB, 3, 2 * FP, BLK), BF16), V((NB, 3, FP, BLK), BF16),
        V((12, NF, 128), F32), V((NY, NF, 128), F32), V((NY, K, 128), F32), V((2, K, 128), F32), V((K, 128), F32),
        V((NX * NC, 8, 128), F32), V((NZ, 8, 128), F32), V((K, 128), BF16),
        V((NX * NC, 8, 128), F32), V((NY, 8, 128), F32), V((NZ, 8, 128), F32),
        V((4, NZ // 2, 64, BLK), BF16), V((4, NX // 2, NZ // 2, 64, BLK), BF16),
        V((4, NX // 2, 48, BLK), BF16), V((4, NZ // 2, NX // 2, 48, BLK), BF16),
        V((4, 32, BLK), BF16), V((4, NZ // 2, 32, BLK), BF16),
        V((4, 32, BLK), BF16), V((4, NX // 2, 32, BLK), BF16),
        V((NZ, 64, BLK), F32), V((NX, 48, BLK), F32),
        dma((CHUNKS,)), dma,
        dma((NY - 1,)), dma((NY - 1,)), dma((NY - 1,)), dma((NY - 1,)),
        dma((NX * NC - 1,)), dma((NX * NC - 1,)), dma((NZ - 1,)), dma((NZ - 1,)),
        dma, dma, dma, dma,
        dma((NX * NC - 1,)), dma((NX * NC - 1,)), dma((NY - 1,)), dma((NY - 1,)), dma((NZ - 1,)), dma((NZ - 1,)),
        dma((4, NX // 2)), dma((4, NX // 2)), dma((4, NZ // 2)), dma((4, NZ // 2)),
        dma((4, NZ // 2)), dma((4, NZ // 2)), dma((4, NX // 2)), dma((4, NX // 2)),
    ]
    nm, img, bas = pl.pallas_call(
        kernel,
        out_shape=(
            jax.ShapeDtypeStruct((3, BLK), F32),
            jax.ShapeDtypeStruct((3, K, BLK), F32),
            jax.ShapeDtypeStruct((3, K, BLK), F32),
        ),
        in_specs=[anyspec, vm, vm, anyspec],
        out_specs=(vm, vm, vm),
        scratch_shapes=scratch,
        compiler_params=pltpu.CompilerParams(
            collective_id=0, has_side_effects=True, vmem_limit_bytes=60 * 1024 * 1024
        ),
    )(x, mean_structure, atom_weight.reshape(1, AL), s)
    return nm, jnp.transpose(img, (1, 0, 2)), jnp.transpose(bas, (1, 0, 2))


def solution(mesh):
    return jax.shard_map(
        per_device,
        mesh=mesh,
        in_specs=(P("frames", None, "atoms"), P(None, "atoms"), P("atoms"), P(None, None, "atoms")),
        out_specs=(
            P(None, ("atoms", "frames")),
            P(None, None, ("atoms", "frames")),
            P(None, None, ("atoms", "frames")),
        ),
        check_vma=False,
    )
```

```python
import jax
import jax.numpy as jnp
from jax import lax
from jax.experimental import pallas as pl
from jax.experimental.pallas import tpu as pltpu
from jax.sharding import PartitionSpec as P

ATOMS = 98304
FRAMES = 1536
NEWTON = 8
NX, NZ, NC, NY = 4, 8, 2, 4
NF = 24
FP = 32
K = 32
AL = ATOMS // NY
BLK = AL // (NX * NZ * NC)
NB = NX * NZ
CHUNKS = 8
CW = AL // CHUNKS
STEP = 512
UNROLL = 8
VLHS = False
F32 = jnp.float32
BF16 = jnp.bfloat16
MESH = pl.DeviceIdType.MESH
HIGHEST = lax.Precision.HIGHEST
STREAMS = tuple((h, d) for h in (0, 1) for d in (1, -1))
NT = (((1,), (1,)), ((), ()))


def steps_of(n, half, direction):
    return n // 2 if (direction == 1) == (half == 0) else n // 2 - 1


def newton(m):
    norm = m[0] * m[0]
    for e in m[1:]:
        norm = norm + e * e
    inv = 1.0 / jnp.sqrt(norm)
    x = [e * inv for e in m]
    for _ in range(NEWTON):
        x00, x01, x02, x10, x11, x12, x20, x21, x22 = x
        cof = [
            x11 * x22 - x12 * x21,
            x12 * x20 - x10 * x22,
            x10 * x21 - x11 * x20,
            x02 * x21 - x01 * x22,
            x00 * x22 - x02 * x20,
            x01 * x20 - x00 * x21,
            x01 * x12 - x02 * x11,
            x02 * x10 - x00 * x12,
            x00 * x11 - x01 * x10,
        ]
        det = x00 * cof[0] + x01 * cof[1] + x02 * cof[2]
        r = 1.0 / det
        x = [0.5 * (a + c * r) for a, c in zip(x, cof)]
    return x


def kernel(
    x_hbm, ms_ref, w_ref, s_hbm, nm_ref, img_ref, g_ref,
    xv, sv, dall, dsend, rot, ex1, ex2, pp, gsq, pba, cpt, gx, gz,
    a1s, a1r, b1s, b1r, a2s, a2r, b2s, b2r, acca, accb,
    xsem, ssem, y1s, y1r, y2s, y2r, px_s, px_r, pp_s, pp_r, dx_s, dx_r,
    gx_s, gx_r, gz_s, gz_r, a1ss, a1rs, b1ss, b1rs, a2ss, a2rs, b2ss, b2rs,
):
    y = lax.axis_index("atoms")
    n = lax.axis_index("frames")
    px = n // (NZ * NC)
    pz = (n // NC) % NZ
    pc = n % NC

    def dev(dx=0, dz=0, dc=0, dy=0):
        tx = (px + (dx + NX)) % NX
        tz = (pz + (dz + NZ)) % NZ
        tc = (pc + dc) % NC
        return ((y + dy) % NY, (tx * NZ + tz) * NC + tc)

    y_peers = [dev(dy=j) for j in range(1, NY)]
    f_peers = [dev(dx=j // (NZ * NC), dz=(j // NC) % NZ, dc=j % NC) for j in range(1, NB * NC)]
    p_peers = [dev(dy=j // (NX * NC), dx=(j // NC) % NX, dc=j % NC) for j in range(1, NX * NC * NY)]
    greet = f_peers + [p_peers[j - 1] for j in range(NX * NC, NX * NC * NY)]
    z_peers = [dev(dz=j) for j in range(1, NZ)]
    partner = dev(dc=1)

    loads = []
    for q in range(CHUNKS):
        cols = pl.ds(q * CW, CW)
        cp = pltpu.make_async_copy(x_hbm.at[:, :, cols], xv.at[:, :, cols], xsem.at[q])
        cp.start()
        loads.append(cp)
    sload = pltpu.make_async_copy(s_hbm, sv, ssem)
    sload.start()

    barrier = pltpu.get_barrier_semaphore()
    for peer in greet:
        pl.semaphore_signal(barrier, inc=1, device_id=peer, device_id_type=MESH)

    def remote(src, dst, ssm, rsm, peer):
        return pltpu.make_async_remote_copy(
            src_ref=src, dst_ref=dst, send_sem=ssm, recv_sem=rsm, device_id=peer, device_id_type=MESH
        )

    pending = []

    def exchange(buf, peers, ssm, rsm):
        copies = []
        for j, peer in enumerate(peers):
            copies.append(remote(buf.at[0], buf.at[j + 1], ssm.at[j], rsm.at[j], peer))
        for c in copies:
            c.start()
        for c in copies:
            c.wait_recv()
        pending.extend(copies)

    lane = lax.broadcasted_iota(jnp.int32, (NF, 128), 1)

    def center_body(q, carry):
        tw, tm = carry
        cols = pl.ds(pl.multiple_of(q * 2048, 2048), 2048)
        wv = w_ref[:, cols]
        return tw + wv, tm + ms_ref[:, cols] * wv

    tw, tm = lax.fori_loop(
        0, AL // 2048, center_body, (jnp.zeros((1, 2048), F32), jnp.zeros((3, 2048), F32))
    )
    tw = jnp.sum(tw, axis=1, keepdims=True)
    tm = jnp.sum(tm, axis=1, keepdims=True)
    lc = tm / tw

    def sums_body(q, acc):
        acc = list(acc)
        cols = pl.ds(pl.multiple_of(q * STEP, STEP), STEP)
        wv = w_ref[:, cols]
        wm = (ms_ref[:, cols] - lc) * wv
        for t in range(STEP // 128):
            lo = t * 128
            sub = pl.ds(pl.multiple_of(q * STEP + lo, 128), 128)
            wt = jnp.broadcast_to(wv[:, lo : lo + 128], (NF, 128))
            mt = [jnp.broadcast_to(wm[i : i + 1, lo : lo + 128], (NF, 128)) for i in range(3)]
            for j in range(3):
                xj = xv[j, :, sub]
                acc[j] = acc[j] + xj * wt
                for i in range(3):
                    acc[3 + i * 3 + j] = acc[3 + i * 3 + j] + xj * mt[i]
        return tuple(acc)

    acc = tuple(jnp.zeros((NF, 128), F32) for _ in range(12))
    per = CW // STEP
    for q in range(CHUNKS):
        loads[q].wait()
        acc = lax.fori_loop(q * per, (q + 1) * per, sums_body, acc)
    sums = [jnp.broadcast_to(jnp.sum(a, axis=1, keepdims=True), (NF, 128)) for a in acc]
    wide = [jnp.broadcast_to(lc[i : i + 1], (NF, 128)) for i in range(3)]
    wide_m = [jnp.broadcast_to(tm[i : i + 1], (NF, 128)) for i in range(3)]
    tile = jnp.broadcast_to(tw, (NF, 128))
    for i in range(3):
        for j in range(3):
            e = 3 * i + j
            tile = jnp.where(lane == e, sums[3 + e], tile)
            tile = jnp.where(lane == 16 + e, sums[j], tile)
            tile = jnp.where(lane == 32 + e, wide[i], tile)
            tile = jnp.where(lane == 48 + e, wide_m[i], tile)
    ex1[0] = tile
    pl.semaphore_wait(barrier, len(greet))
    exchange(ex1, y_peers, y1s, y1r)

    slots = [ex1[j] for j in range(NY)]
    tsum = slots[0] + slots[1] + slots[2] + slots[3]
    inv_total = 1.0 / jnp.broadcast_to(tsum[:, 127:128], (NF, 128))
    tsum = tsum * inv_total
    mrep = pltpu.roll(tsum, 128 - 48, 1)
    packed = None
    for p in slots:
        t = p + (pltpu.roll(p, 128 - 32, 1) - mrep) * pltpu.roll(p, 128 - 16, 1)
        packed = t if packed is None else packed + t
    packed = packed * inv_total
    r = newton([jnp.broadcast_to(packed[:, q : q + 1], (NF, 128)) for q in range(9)])
    fc = [jnp.broadcast_to(tsum[:, 16 + j : 17 + j], (NF, 128)) for j in range(3)]
    mc = [jnp.broadcast_to(tsum[:, 48 + 3 * i : 49 + 3 * i], (NF, 128)) for i in range(3)]
    for q in range(9):
        rot[q] = r[q]
    for i in range(3):
        off = r[3 * i] * fc[0] + r[3 * i + 1] * fc[1] + r[3 * i + 2] * fc[2]
        rot[9 + i] = mc[i] - off

    sload.wait()

    def move_body(own):
        def body(g, acc):
            core = pc if own else 1 - pc
            for i in range(3):
                vs, ss = [], []
                for u in range(UNROLL):
                    b = g * UNROLL + u
                    base = (b * NC + core) * BLK
                    pieces = []
                    for t in range(BLK // 128):
                        sub = pl.ds(pl.multiple_of(base + t * 128, 128), 128)
                        v = rot[3 * i] * xv[0, :, sub] + rot[3 * i + 1] * xv[1, :, sub] + rot[3 * i + 2] * xv[2, :, sub]
                        v = v + rot[9 + i] - jnp.broadcast_to(ms_ref[i : i + 1, sub], (NF, 128))
                        pieces.append(v)
                    v = jnp.concatenate(pieces, axis=1)
                    v = jnp.concatenate([v, jnp.zeros((FP - NF, BLK), F32)], axis=0).astype(BF16)
                    if own:
                        dall[b, i, 0:FP, :] = v
                    else:
                        dsend[b, i] = v
                    vs.append(v)
                    ss.append(sv[i, :, pl.ds(pl.multiple_of(base, 128), BLK)])
                vs = jnp.concatenate(vs, axis=1)
                ss = jnp.concatenate(ss, axis=1)
                if VLHS:
                    acc = acc + lax.dot_general(vs, ss, NT, preferred_element_type=F32)
                else:
                    acc = acc + lax.dot_general(ss, vs, NT, preferred_element_type=F32)
            return acc

        return body

    pacc = lax.fori_loop(0, NB // UNROLL, move_body(False), jnp.zeros((K, FP), F32))
    dcopy = remote(dsend, dall.at[:, :, FP : 2 * FP, :], dx_s, dx_r, partner)
    dcopy.start()
    pacc = lax.fori_loop(0, NB // UNROLL, move_body(True), pacc)
    if VLHS:
        pacc = pacc.T

    ex2[0] = jnp.zeros((K, 128), F32)
    ex2[0, :, 0:FP] = pacc
    exchange(ex2, y_peers, y2s, y2r)
    ptot = ex2[0] + ex2[1] + ex2[2] + ex2[3]
    pp[0] = ptot
    pcopy = remote(pp.at[0], pp.at[1], pp_s, pp_r, partner)
    pcopy.start()
    rows = lax.broadcasted_iota(jnp.int32, (K, 128), 0)
    lanes = lax.broadcasted_iota(jnp.int32, (K, 128), 1)
    col = jnp.broadcast_to(jnp.sum(ptot, axis=1, keepdims=True), (K, 128))
    row = jnp.sum(jnp.where(rows == lanes, col, 0.0), axis=0, keepdims=True)
    pba[0] = row
    exchange(pba, f_peers, px_s, px_r)
    row = jnp.broadcast_to(jnp.sum(pba[...], axis=0), (K, 128))
    pbar = jnp.sum(jnp.where(rows == lanes, row, 0.0), axis=1, keepdims=True) / FRAMES
    pcopy.wait_recv()
    other = pltpu.roll(pp[1], FP, 1)
    both = jnp.where(lanes < FP, ptot, other) - pbar
    cpt[...] = both.astype(BF16)
    dcopy.wait_recv()

    erow = lax.broadcasted_iota(jnp.int32, (16, 2 * FP), 0)
    ones = [jnp.where(erow == i, 1.0, 0.0).astype(BF16) for i in range(3)]

    def mm(lhs, rhs):
        return jnp.dot(lhs, rhs, preferred_element_type=F32)

    def term_a(dest, h, emit):
        def body(q, c):
            blk = dest * NZ + h * (NZ // 2) + q
            for i in range(2):
                emit(q, i, mm(cpt[:, 0 : 2 * FP], dall[blk, i]))
            return c

        lax.fori_loop(0, NZ // 2, body, 0)

    def term_b(dest, h, emit):
        def body(q, c):
            blk = (h * (NX // 2) + q) * NZ + dest
            emit(q, 0, mm(cpt[:, 0 : 2 * FP], dall[blk, 2]))
            sh = mm(ones[0], dall[blk, 0]) + mm(ones[1], dall[blk, 1]) + mm(ones[2], dall[blk, 2])
            emit(q, 1, sh)
            return c

        lax.fori_loop(0, NX // 2, body, 0)

    def rowslice(i):
        return slice(32 * i, 32 * i + 32)

    def brow(i):
        return slice(0, 32) if i == 0 else slice(32, 48)

    class Stage:
        def __init__(self, length, pos, sbuf, rbuf, ssm, rsm, fill, peer_of, cut):
            self.length, self.pos, self.sbuf, self.rbuf = length, pos, sbuf, rbuf
            self.ssm, self.rsm, self.fill, self.peer_of, self.cut = ssm, rsm, fill, peer_of, cut
            self.copies = {}

        def send(self, st, s):
            h, d = STREAMS[st]
            total_steps = steps_of(self.length, h, d)
            if s >= total_steps:
                return
            dest = (self.pos + (d * (total_steps - s) + self.length)) % self.length
            if s == 0:
                src = self.sbuf.at[st]
                self.fill(src, dest, h, False)
            else:
                self.copies[st, s - 1].wait_recv()
                src = self.rbuf.at[st, s - 1]
                self.fill(src, dest, h, True)
            c = remote(
                self.cut(src, h), self.cut(self.rbuf.at[st, s], h), self.ssm.at[st, s], self.rsm.at[st, s],
                self.peer_of(d),
            )
            c.start()
            pending.append(c)
            self.copies[st, s] = c

        def finals(self, h):
            out = []
            for st, (hh, d) in enumerate(STREAMS):
                if hh == h:
                    s = steps_of(self.length, h, d) - 1
                    self.copies[st, s].wait_recv()
                    out.append(self.rbuf.at[st, s])
            return out

    def fill_a1(ref, dest, h, add):
        def emit(q, i, t):
            if add:
                t = t + ref[q, rowslice(i), :].astype(F32)
            ref[q, rowslice(i), :] = t.astype(BF16)

        term_a(dest, h, emit)

    def fill_b1(ref, dest, h, add):
        def emit(q, i, t):
            if add:
                t = t + ref[q, brow(i), :].astype(F32)
            ref[q, brow(i), :] = t.astype(BF16)

        term_b(dest, h, emit)

    def fill_a2(ref, dest, h, add):
        t = acca[dest, rowslice(h), :]
        if add:
            t = t + ref[...].astype(F32)
        ref[...] = t.astype(BF16)

    def fill_b2(ref, dest, h, add):
        if h == 0:
            t = accb[dest, 0:32, :]
            if add:
                t = t + ref[...].astype(F32)
            ref[...] = t.astype(BF16)
        else:
            t = accb[dest, 32:48, :]
            if add:
                t = t + ref[0:16, :].astype(F32)
            ref[0:16, :] = t.astype(BF16)

    def whole(ref, h):
        return ref

    def cut_b2(ref, h):
        return ref if h == 0 else ref.at[0:16, :]

    x_dir = {1: dev(dx=1), -1: dev(dx=-1)}
    z_dir = {1: dev(dz=1), -1: dev(dz=-1)}
    sa1 = Stage(NX, px, a1s, a1r, a1ss, a1rs, fill_a1, x_dir.get, whole)
    sb1 = Stage(NZ, pz, b1s, b1r, b1ss, b1rs, fill_b1, z_dir.get, whole)
    sa2 = Stage(NZ, pz, a2s, a2r, a2ss, a2rs, fill_a2, z_dir.get, whole)
    sb2 = Stage(NX, px, b2s, b2r, b2ss, b2rs, fill_b2, x_dir.get, cut_b2)

    order = (0, 3, 2, 1)
    for st in order:
        sa1.send(st, 0)
        sb1.send(st, 0)
    for st in order:
        sb1.send(st, 1)
    for st in order:
        sa1.send(st, 1)
    for st in order:
        sb1.send(st, 2)
    for st in order:
        sb1.send(st, 3)

    for h in (0, 1):
        f0, f1 = sa1.finals(h)

        def emit(q, i, t, f0=f0, f1=f1, h=h):
            t = t + f0[q, rowslice(i), :].astype(F32) + f1[q, rowslice(i), :].astype(F32)
            acca[h * (NZ // 2) + q, rowslice(i), :] = t

        term_a(px, h, emit)
    for st in order:
        sa2.send(st, 0)
    for h in (0, 1):
        f0, f1 = sb1.finals(h)

        def emit(q, i, t, f0=f0, f1=f1, h=h):
            t = t + f0[q, brow(i), :].astype(F32) + f1[q, brow(i), :].astype(F32)
            accb[h * (NX // 2) + q, brow(i), :] = t

        term_b(pz, h, emit)
    for st in order:
        sb2.send(st, 0)
    for st in order:
        sa2.send(st, 1)
    for st in order:
        sb2.send(st, 1)
    for st in order:
        sa2.send(st, 2)
    for st in order:
        sa2.send(st, 3)

    inv_f = 1.0 / FRAMES
    f0, f1 = sb2.finals(0)
    img2 = (accb[px, 0:32, :] + f0[...].astype(F32) + f1[...].astype(F32)) * inv_f
    f0, f1 = sb2.finals(1)
    shift = accb[px, 32:48, :] + f0[0:16, :].astype(F32) + f1[0:16, :].astype(F32)
    own = pl.ds(pl.multiple_of(n * BLK, 128), BLK)
    nm_ref[...] = ms_ref[:, own] + shift[0:3] * inv_f
    imgs = []
    for h in (0, 1):
        f0, f1 = sa2.finals(h)
        imgs.append((acca[pz, rowslice(h), :] + f0[...].astype(F32) + f1[...].astype(F32)) * inv_f)
    imgs.append(img2)
    g = None
    for i in range(3):
        img_ref[i] = imgs[i]
        t = lax.dot_general(imgs[i], imgs[i], NT, preferred_element_type=F32, precision=HIGHEST)
        g = t if g is None else g + t
    gsq[...] = jnp.zeros((K, 128), F32)
    gsq[:, 0:K] = g
    v = gsq[0:8, :]
    for q in range(1, 4):
        v = v + pltpu.roll(gsq[8 * q : 8 * q + 8, :], 32 * q, 1)
    gx[0] = v
    exchange(gx, p_peers, gx_s, gx_r)
    gz[0] = jnp.sum(gx[...], axis=0)
    exchange(gz, z_peers, gz_s, gz_r)
    v = gz[0]
    for j in range(1, NZ):
        v = v + gz[j]
    g_ref[...] = v / (3 * ATOMS)

    for c in pending + [dcopy, pcopy]:
        c.wait_send()


def finish(nm_in, img_in, g_ref, nm_ref, img_ref, bas_ref):
    rows = lax.broadcasted_iota(jnp.int32, (K, 128), 0)
    lanes = lax.broadcasted_iota(jnp.int32, (K, 128), 1)
    v = g_ref[...]
    m = jnp.concatenate([v] + [pltpu.roll(v, 128 - 32 * q, 1) for q in range(1, 4)], axis=0)
    m = jnp.where(lanes < K, m, jnp.where(lanes - K == rows, 1.0, 0.0))
    for j in range(K - 1):
        prow = jnp.broadcast_to(m[j : j + 1, :], (K, 128))
        pcol = jnp.broadcast_to(m[:, j : j + 1], (K, 128))
        piv = 1.0 / pcol[j : j + 1, :]
        m = jnp.where(rows > j, m - pcol * (prow * piv), m)
    diag = jnp.sum(jnp.where(rows == lanes, m, 0.0), axis=1, keepdims=True)
    linv = pltpu.roll(m, 128 - K, 1) * (1.0 / jnp.sqrt(diag))
    linv = linv[:, 0:K]
    for i in range(3):
        bas_ref[i] = jnp.dot(linv, img_in[i], preferred_element_type=F32, precision=HIGHEST)
        img_ref[i] = img_in[i]
    nm_ref[...] = nm_in[...]


def per_device(frames, mean_structure, atom_weight, subspace):
    x = jnp.transpose(frames, (1, 0, 2))
    s = jnp.transpose(subspace, (1, 0, 2))
    vm = pl.BlockSpec(memory_space=pltpu.VMEM)
    anyspec = pl.BlockSpec(memory_space=pl.ANY)
    dma = pltpu.SemaphoreType.DMA
    V = pltpu.VMEM
    scratch = [
        V((3, NF, AL), F32), V((3, K, AL), BF16), V((NB, 3, 2 * FP, BLK), BF16), V((NB, 3, FP, BLK), BF16),
        V((12, NF, 128), F32), V((NY, NF, 128), F32), V((NY, K, 128), F32), V((2, K, 128), F32), V((K, 128), F32),
        V((NB * NC, 1, 128), F32), V((K, 128), BF16),
        V((NX * NC * NY, 8, 128), F32), V((NZ, 8, 128), F32),
        V((4, NZ // 2, 64, BLK), BF16), V((4, NX // 2, NZ // 2, 64, BLK), BF16),
        V((4, NX // 2, 48, BLK), BF16), V((4, NZ // 2, NX // 2, 48, BLK), BF16),
        V((4, 32, BLK), BF16), V((4, NZ // 2, 32, BLK), BF16),
        V((4, 32, BLK), BF16), V((4, NX // 2, 32, BLK), BF16),
        V((NZ, 64, BLK), F32), V((NX, 48, BLK), F32),
        dma((CHUNKS,)), dma,
        dma((NY - 1,)), dma((NY - 1,)), dma((NY - 1,)), dma((NY - 1,)),
        dma((NB * NC - 1,)), dma((NB * NC - 1,)),
        dma, dma, dma, dma,
        dma((NX * NC * NY - 1,)), dma((NX * NC * NY - 1,)), dma((NZ - 1,)), dma((NZ - 1,)),
        dma((4, NX // 2)), dma((4, NX // 2)), dma((4, NZ // 2)), dma((4, NZ // 2)),
        dma((4, NZ // 2)), dma((4, NZ // 2)), dma((4, NX // 2)), dma((4, NX // 2)),
    ]
    shapes = [(3, BLK), (3, K, BLK), (8, 128)]
    nm, img, gram = pl.pallas_call(
        kernel,
        out_shape=tuple(jax.ShapeDtypeStruct(d, F32) for d in shapes),
        in_specs=[anyspec, vm, vm, anyspec],
        out_specs=(vm, vm, vm),
        scratch_shapes=scratch,
        compiler_params=pltpu.CompilerParams(
            collective_id=0, has_side_effects=True, vmem_limit_bytes=60 * 1024 * 1024
        ),
    )(x, mean_structure, atom_weight.reshape(1, AL), s)
    shapes = [(3, BLK), (3, K, BLK), (3, K, BLK)]
    nm, img, bas = pl.pallas_call(
        finish,
        out_shape=tuple(jax.ShapeDtypeStruct(d, F32) for d in shapes),
        in_specs=[vm, vm, vm],
        out_specs=(vm, vm, vm),
    )(nm, img, gram)
    return nm, jnp.transpose(img, (1, 0, 2)), jnp.transpose(bas, (1, 0, 2))


def solution(mesh):
    return jax.shard_map(
        per_device,
        mesh=mesh,
        in_specs=(P("frames", None, "atoms"), P(None, "atoms"), P("atoms"), P(None, None, "atoms")),
        out_specs=(
            P(None, ("atoms", "frames")),
            P(None, None, ("atoms", "frames")),
            P(None, None, ("atoms", "frames")),
        ),
        check_vma=False,
    )
```

```python
import jax
import jax.numpy as jnp
from jax import lax
from jax.experimental import pallas as pl
from jax.experimental.pallas import tpu as pltpu
from jax.sharding import PartitionSpec as P

ATOMS = 98304
FRAMES = 1536
NEWTON = 8
NX, NZ, NC, NY = 4, 8, 2, 4
NF = 24
FP = 32
K = 32
AL = ATOMS // NY
BLK = AL // (NX * NZ * NC)
NB = NX * NZ
CHUNKS = 8
CW = AL // CHUNKS
STEP = 512
UNROLL = 8
VLHS = False
F32 = jnp.float32
BF16 = jnp.bfloat16
MESH = pl.DeviceIdType.MESH
HIGHEST = lax.Precision.HIGHEST
PARTS = ((3, 4), (5, 2), (6, 1), (7, 0))
NT = (((1,), (1,)), ((), ()))


def steps_of(n, half, direction):
    return n // 2 if (direction == 1) == (half == 0) else n // 2 - 1


def newton(m):
    norm = m[0] * m[0]
    for e in m[1:]:
        norm = norm + e * e
    inv = 1.0 / jnp.sqrt(norm)
    x = [e * inv for e in m]
    for _ in range(NEWTON):
        x00, x01, x02, x10, x11, x12, x20, x21, x22 = x
        cof = [
            x11 * x22 - x12 * x21,
            x12 * x20 - x10 * x22,
            x10 * x21 - x11 * x20,
            x02 * x21 - x01 * x22,
            x00 * x22 - x02 * x20,
            x01 * x20 - x00 * x21,
            x01 * x12 - x02 * x11,
            x02 * x10 - x00 * x12,
            x00 * x11 - x01 * x10,
        ]
        det = x00 * cof[0] + x01 * cof[1] + x02 * cof[2]
        r = 1.0 / det
        x = [0.5 * (a + c * r) for a, c in zip(x, cof)]
    return x


def kernel(
    x_hbm, ms_hbm, w_hbm, s_hbm, nm_ref, img_ref, g_ref,
    ms_ref, w_ref, xv, sv, dall, dsend, rot, ex1, ex2, pp, gsq, pba, cpt, gx, gz,
    a1s, a1r, b1s, b1r, a2s, a2r, b2s, b2r, acca, accb, taf, tbf,
    msem, wsem, xsem, ssem, y1s, y1r, y2s, y2r, px_s, px_r, pp_s, pp_r, dx_s, dx_r,
    gx_s, gx_r, gz_s, gz_r, a1ss, a1rs, b1ss, b1rs, a2ss, a2rs, b2ss, b2rs,
):
    y = lax.axis_index("atoms")
    n = lax.axis_index("frames")
    px = n // (NZ * NC)
    pz = (n // NC) % NZ
    pc = n % NC

    def dev(dx=0, dz=0, dc=0, dy=0):
        tx = (px + (dx + NX)) % NX
        tz = (pz + (dz + NZ)) % NZ
        tc = (pc + dc) % NC
        return ((y + dy) % NY, (tx * NZ + tz) * NC + tc)

    y_peers = [dev(dy=j) for j in range(1, NY)]
    f_peers = [dev(dx=j // (NZ * NC), dz=(j // NC) % NZ, dc=j % NC) for j in range(1, NB * NC)]
    p_peers = [dev(dy=j // (NX * NC), dx=(j // NC) % NX, dc=j % NC) for j in range(1, NX * NC * NY)]
    greet = f_peers + [p_peers[j - 1] for j in range(NX * NC, NX * NC * NY)]
    z_peers = [dev(dz=j) for j in range(1, NZ)]
    partner = dev(dc=1)

    mload = pltpu.make_async_copy(ms_hbm, ms_ref, msem)
    wload = pltpu.make_async_copy(w_hbm, w_ref, wsem)
    wload.start()
    mload.start()
    loads = []
    for q in range(CHUNKS):
        cols = pl.ds(q * CW, CW)
        cp = pltpu.make_async_copy(x_hbm.at[:, :, cols], xv.at[:, :, cols], xsem.at[q])
        loads.append(cp)
    for cp in loads[:2]:
        cp.start()
    sload = pltpu.make_async_copy(s_hbm, sv, ssem)

    barrier = pltpu.get_barrier_semaphore()
    for peer in greet:
        pl.semaphore_signal(barrier, inc=1, device_id=peer, device_id_type=MESH)

    def remote(src, dst, ssm, rsm, peer):
        return pltpu.make_async_remote_copy(
            src_ref=src, dst_ref=dst, send_sem=ssm, recv_sem=rsm, device_id=peer, device_id_type=MESH
        )

    pending = []

    def exchange(buf, peers, ssm, rsm):
        copies = []
        for j, peer in enumerate(peers):
            copies.append(remote(buf.at[0], buf.at[j + 1], ssm.at[j], rsm.at[j], peer))
        for c in copies:
            c.start()
        for c in copies:
            c.wait_recv()
        pending.extend(copies)

    lane = lax.broadcasted_iota(jnp.int32, (NF, 128), 1)

    wload.wait()
    mload.wait()
    for cp in loads[2:]:
        cp.start()
    lc = jnp.sum(ms_ref[:, 0:2048], axis=1, keepdims=True) * (1.0 / 2048)

    def sums_body(q, acc):
        acc = list(acc)
        tw, tm = acc[12:]
        cols = pl.ds(pl.multiple_of(q * STEP, STEP), STEP)
        wv = w_ref[:, cols]
        wm = (ms_ref[:, cols] - lc) * wv
        acc[12:] = [tw + wv, tm + wm]
        for t in range(STEP // 128):
            lo = t * 128
            sub = pl.ds(pl.multiple_of(q * STEP + lo, 128), 128)
            wt = jnp.broadcast_to(wv[:, lo : lo + 128], (NF, 128))
            mt = [jnp.broadcast_to(wm[i : i + 1, lo : lo + 128], (NF, 128)) for i in range(3)]
            for j in range(3):
                xj = xv[j, :, sub]
                acc[j] = acc[j] + xj * wt
                for i in range(3):
                    acc[3 + i * 3 + j] = acc[3 + i * 3 + j] + xj * mt[i]
        return tuple(acc)

    acc = tuple(jnp.zeros((NF, 128), F32) for _ in range(12))
    acc += (jnp.zeros((1, STEP), F32), jnp.zeros((3, STEP), F32))
    per = CW // STEP
    for q in range(CHUNKS):
        if q == CHUNKS - 1:
            sload.start()
        loads[q].wait()
        acc = lax.fori_loop(q * per, (q + 1) * per, sums_body, acc)
    tw = jnp.sum(acc[12], axis=1, keepdims=True)
    tm = jnp.sum(acc[13], axis=1, keepdims=True) + lc * tw
    sums = [jnp.broadcast_to(jnp.sum(a, axis=1, keepdims=True), (NF, 128)) for a in acc[:12]]
    wide = [jnp.broadcast_to(lc[i : i + 1], (NF, 128)) for i in range(3)]
    wide_m = [jnp.broadcast_to(tm[i : i + 1], (NF, 128)) for i in range(3)]
    tile = jnp.broadcast_to(tw, (NF, 128))
    for i in range(3):
        for j in range(3):
            e = 3 * i + j
            tile = jnp.where(lane == e, sums[3 + e], tile)
            tile = jnp.where(lane == 16 + e, sums[j], tile)
            tile = jnp.where(lane == 32 + e, wide[i], tile)
            tile = jnp.where(lane == 48 + e, wide_m[i], tile)
    ex1[0] = tile
    pl.semaphore_wait(barrier, len(greet))
    exchange(ex1, y_peers, y1s, y1r)

    slots = [ex1[j] for j in range(NY)]
    tsum = slots[0] + slots[1] + slots[2] + slots[3]
    inv_total = 1.0 / jnp.broadcast_to(tsum[:, 127:128], (NF, 128))
    tsum = tsum * inv_total
    mrep = pltpu.roll(tsum, 128 - 48, 1)
    packed = None
    for p in slots:
        t = p + (pltpu.roll(p, 128 - 32, 1) - mrep) * pltpu.roll(p, 128 - 16, 1)
        packed = t if packed is None else packed + t
    packed = packed * inv_total
    r = newton([jnp.broadcast_to(packed[:, q : q + 1], (NF, 128)) for q in range(9)])
    fc = [jnp.broadcast_to(tsum[:, 16 + j : 17 + j], (NF, 128)) for j in range(3)]
    mc = [jnp.broadcast_to(tsum[:, 48 + 3 * i : 49 + 3 * i], (NF, 128)) for i in range(3)]
    for q in range(9):
        rot[q] = r[q]
    for i in range(3):
        off = r[3 * i] * fc[0] + r[3 * i + 1] * fc[1] + r[3 * i + 2] * fc[2]
        rot[9 + i] = mc[i] - off

    sload.wait()

    def move_body(own):
        def body(g, acc):
            core = pc if own else 1 - pc
            for i in range(3):
                vs, ss = [], []
                for u in range(UNROLL):
                    b = g * UNROLL + u
                    base = (b * NC + core) * BLK
                    pieces = []
                    for t in range(BLK // 128):
                        sub = pl.ds(pl.multiple_of(base + t * 128, 128), 128)
                        v = rot[3 * i] * xv[0, :, sub] + rot[3 * i + 1] * xv[1, :, sub] + rot[3 * i + 2] * xv[2, :, sub]
                        v = v + rot[9 + i] - jnp.broadcast_to(ms_ref[i : i + 1, sub], (NF, 128))
                        pieces.append(v)
                    v = jnp.concatenate(pieces, axis=1)
                    v = jnp.concatenate([v, jnp.zeros((FP - NF, BLK), F32)], axis=0).astype(BF16)
                    if own:
                        dall[b, i, 0:FP, :] = v
                    else:
                        dsend[b, i] = v
                    vs.append(v)
                    ss.append(sv[i, :, pl.ds(pl.multiple_of(base, 128), BLK)])
                vs = jnp.concatenate(vs, axis=1)
                ss = jnp.concatenate(ss, axis=1)
                if VLHS:
                    acc = acc + lax.dot_general(vs, ss, NT, preferred_element_type=F32)
                else:
                    acc = acc + lax.dot_general(ss, vs, NT, preferred_element_type=F32)
            return acc

        return body

    pacc = lax.fori_loop(0, NB // UNROLL, move_body(False), jnp.zeros((K, FP), F32))
    dcopy = remote(dsend, dall.at[:, :, FP : 2 * FP, :], dx_s, dx_r, partner)
    dcopy.start()
    pacc = lax.fori_loop(0, NB // UNROLL, move_body(True), pacc)
    if VLHS:
        pacc = pacc.T

    ex2[0] = jnp.zeros((K, 128), F32)
    ex2[0, :, 0:FP] = pacc
    exchange(ex2, y_peers, y2s, y2r)
    ptot = ex2[0] + ex2[1] + ex2[2] + ex2[3]
    pp[0] = ptot
    pcopy = remote(pp.at[0], pp.at[1], pp_s, pp_r, partner)
    pcopy.start()
    rows = lax.broadcasted_iota(jnp.int32, (K, 128), 0)
    lanes = lax.broadcasted_iota(jnp.int32, (K, 128), 1)
    col = jnp.broadcast_to(jnp.sum(ptot, axis=1, keepdims=True), (K, 128))
    row = jnp.sum(jnp.where(rows == lanes, col, 0.0), axis=0, keepdims=True)
    pba[0] = row
    exchange(pba, f_peers, px_s, px_r)
    row = jnp.broadcast_to(jnp.sum(pba[...], axis=0), (K, 128))
    pbar = jnp.sum(jnp.where(rows == lanes, row, 0.0), axis=1, keepdims=True) / FRAMES
    pcopy.wait_recv()
    other = pltpu.roll(pp[1], FP, 1)
    both = jnp.where(lanes < FP, ptot, other) - pbar
    cpt[...] = both.astype(BF16)
    dcopy.wait_recv()

    erow = lax.broadcasted_iota(jnp.int32, (16, 2 * FP), 0)
    ones = [jnp.where(erow == i, 1.0, 0.0).astype(BF16) for i in range(6)]
    coef = cpt[:, 0 : 2 * FP]
    coef2 = [jnp.concatenate([coef, ones[3 * q + 2]], axis=0) for q in range(2)]

    def mm(lhs, rhs):
        return jnp.dot(lhs, rhs, preferred_element_type=F32)

    def zblk(g, q):
        return (pz + PARTS[g][q]) % NZ

    def term_a(dest, g, emit):
        for q in range(2):
            blk = dest * NZ + zblk(g, q)
            for i in range(2):
                emit(q, i, mm(coef, dall[blk, i]))

    def term_b(dest, h, ref):
        tail = None
        for q in range(2):
            blk = (h * (NX // 2) + q) * NZ + dest
            t = mm(coef2[q], dall[blk, 2])
            ref[32 * q : 32 * q + 32, :] = t[0:32].astype(ref.dtype)
            t = t[32:48] + (mm(ones[3 * q], dall[blk, 0]) + mm(ones[3 * q + 1], dall[blk, 1]))
            tail = t if tail is None else tail + t
        ref[64:80, :] = tail.astype(ref.dtype)

    def rowslice(i):
        return slice(32 * i, 32 * i + 32)

    def store(ref, rows_of):
        def emit(q, i, t):
            ref[q, rows_of(i), :] = t.astype(ref.dtype)

        return emit

    class Stage:
        def __init__(self, length, pos, parts, sbuf, rbuf, ssm, rsm, fill, peer_of, cut):
            self.length, self.pos, self.sbuf, self.rbuf = length, pos, sbuf, rbuf
            self.ssm, self.rsm, self.fill, self.peer_of, self.cut = ssm, rsm, fill, peer_of, cut
            self.streams = tuple((h, d) for h in range(parts) for d in (1, -1))
            self.copies = {}

        def steps(self, st):
            h, d = self.streams[st]
            return steps_of(self.length, h % 2, d)

        def dest(self, st, s):
            h, d = self.streams[st]
            return (self.pos + (d * (self.steps(st) - s) + self.length)) % self.length

        def send(self, st, s):
            h, d = self.streams[st]
            if s >= self.steps(st):
                return
            if s == 0:
                src = self.sbuf.at[st]
            else:
                self.copies[st, s - 1].wait_recv()
                src = self.rbuf.at[st, s - 1]
            self.fill(src, st, s)
            c = remote(
                self.cut(src, h), self.cut(self.rbuf.at[st, s], h), self.ssm.at[st, s], self.rsm.at[st, s],
                self.peer_of(d),
            )
            c.start()
            pending.append(c)
            self.copies[st, s] = c

        def finals(self, h):
            out = []
            for st, (hh, d) in enumerate(self.streams):
                if hh == h:
                    s = self.steps(st) - 1
                    self.copies[st, s].wait_recv()
                    out.append(self.rbuf.at[st, s])
            return out

    def fill_a1(ref, st, s):
        g = st // 2
        if s == 0:
            term_a(sa1.dest(st, 0), g, store(ref, rowslice))
        else:
            ref[...] = (taf[g] + ref[...].astype(F32)).astype(BF16)

    def fill_b1(ref, st, s):
        if s == 0:
            term_b(sb1.dest(st, 0), st // 2, ref)
        else:
            ref[...] = (tbf[st, s - 1] + ref[...].astype(F32)).astype(BF16)

    def fill_a2(ref, st, s):
        t = acca[sa2.dest(st, s), rowslice(st // 2), :]
        if s:
            t = t + ref[...].astype(F32)
        ref[...] = t.astype(BF16)

    def fill_b2(ref, st, s):
        e = sb2.dest(st, s)
        if st // 2 == 0:
            size, t = 32, accb[e // 2, pl.ds(pl.multiple_of(e % 2 * 32, 32), 32), :]
        else:
            size, t = 16, accb[e // 2, 64:80, :]
        if s:
            t = t + ref[0:size, :].astype(F32)
        ref[0:size, :] = t.astype(BF16)

    def whole(ref, h):
        return ref

    def cut_b2(ref, h):
        return ref if h == 0 else ref.at[0:16, :]

    x_dir = {1: dev(dx=1), -1: dev(dx=-1)}
    z_dir = {1: dev(dz=1), -1: dev(dz=-1)}
    sa1 = Stage(NX, px, 4, a1s, a1r, a1ss, a1rs, fill_a1, x_dir.get, whole)
    sb1 = Stage(NZ, pz, 2, b1s, b1r, b1ss, b1rs, fill_b1, z_dir.get, whole)
    sa2 = Stage(NZ, pz, 2, a2s, a2r, a2ss, a2rs, fill_a2, z_dir.get, whole)
    sb2 = Stage(NX, px, 2, b2s, b2r, b2ss, b2rs, fill_b2, x_dir.get, cut_b2)

    order = (0, 3, 2, 1)
    for st in order:
        sa1.send(st, 0)
        sb1.send(st, 0)
    sa1.send(4, 0)
    sa1.send(7, 0)
    for s in range(1, NZ // 2):
        for st in order:
            if s < sb1.steps(st):
                term_b(sb1.dest(st, s), st // 2, tbf.at[st, s - 1])
        if s == 1:
            term_a(sa1.dest(0, 1), 0, store(taf.at[0], rowslice))
            term_a(sa1.dest(3, 1), 1, store(taf.at[1], rowslice))
            for st in order:
                sb1.send(st, 1)
            sa1.send(0, 1)
            sa1.send(3, 1)
            sa1.send(6, 0)
            sa1.send(5, 0)
            term_a(sa1.dest(4, 1), 2, store(taf.at[2], rowslice))
            term_a(sa1.dest(7, 1), 3, store(taf.at[3], rowslice))

    def own_a(g):
        def emit(q, i, t):
            acca[zblk(g, q), rowslice(i), :] = t

        term_a(px, g, emit)

    def fin_a(g):
        f0, f1 = sa1.finals(g)
        for q in range(2):
            z = zblk(g, q)
            acca[z] = acca[z] + (f0[q].astype(F32) + f1[q].astype(F32))

    own_a(0)
    own_a(1)
    for st in order:
        sb1.send(st, 2)
    sa1.send(4, 1)
    sa1.send(7, 1)
    own_a(2)
    own_a(3)
    for h in (0, 1):
        term_b(pz, h, accb.at[h])
    fin_a(0)
    fin_a(1)
    for st in order:
        sa2.send(st, 0)
    for st in order:
        sb1.send(st, 3)
    for st in (0, 3, 2):
        sa2.send(st, 1)
    for h in (0, 1):
        f0, f1 = sb1.finals(h)
        accb[h] = accb[h] + (f0[...].astype(F32) + f1[...].astype(F32))
    for st in order:
        sb2.send(st, 0)
    fin_a(2)
    fin_a(3)
    sa2.send(1, 1)
    for st in order:
        sa2.send(st, 2)
    for st in order:
        sb2.send(st, 1)
    for st in order:
        sa2.send(st, 3)

    inv_f = 1.0 / FRAMES
    f0, f1 = sb2.finals(0)
    img2 = (accb[px // 2, pl.ds(pl.multiple_of(px % 2 * 32, 32), 32), :] + f0[...].astype(F32) + f1[...].astype(F32)) * inv_f
    f0, f1 = sb2.finals(1)
    shift = accb[px // 2, 64:80, :] + f0[0:16, :].astype(F32) + f1[0:16, :].astype(F32)
    shift = jnp.where(px % 2 == 0, shift[0:3], shift[3:6])
    own = pl.ds(pl.multiple_of(n * BLK, 128), BLK)
    nm_ref[...] = ms_ref[:, own] + shift * inv_f
    imgs = []
    for h in (0, 1):
        f0, f1 = sa2.finals(h)
        imgs.append((acca[pz, rowslice(h), :] + f0[...].astype(F32) + f1[...].astype(F32)) * inv_f)
    imgs.append(img2)
    g = None
    for i in range(3):
        img_ref[i] = imgs[i]
        t = lax.dot_general(imgs[i], imgs[i], NT, preferred_element_type=F32, precision=HIGHEST)
        g = t if g is None else g + t
    gsq[...] = jnp.zeros((K, 128), F32)
    gsq[:, 0:K] = g
    v = gsq[0:8, :]
    for q in range(1, 4):
        v = v + pltpu.roll(gsq[8 * q : 8 * q + 8, :], 32 * q, 1)
    gx[0] = v
    exchange(gx, p_peers, gx_s, gx_r)
    gz[0] = jnp.sum(gx[...], axis=0)
    exchange(gz, z_peers, gz_s, gz_r)
    v = gz[0]
    for j in range(1, NZ):
        v = v + gz[j]
    g_ref[...] = v / (3 * ATOMS)

    for c in pending + [dcopy, pcopy]:
        c.wait_send()


def finish(nm_in, img_in, g_ref, nm_ref, img_ref, bas_ref):
    rows = lax.broadcasted_iota(jnp.int32, (K, 128), 0)
    lanes = lax.broadcasted_iota(jnp.int32, (K, 128), 1)
    v = g_ref[...]
    m = jnp.concatenate([v] + [pltpu.roll(v, 128 - 32 * q, 1) for q in range(1, 4)], axis=0)
    m = jnp.where(lanes < K, m, jnp.where(lanes - K == rows, 1.0, 0.0))
    for j in range(0, K, 2):
        r0 = m[j : j + 1, :]
        r1 = m[j + 1 : j + 2, :]
        c0 = jnp.broadcast_to(m[:, j : j + 1], (K, 128))
        c1 = jnp.broadcast_to(m[:, j + 1 : j + 2], (K, 128))
        ia = 1.0 / c0[j : j + 1, :]
        ratio = c0[j + 1 : j + 2, :] * ia
        r1 = r1 - ratio * r0
        u1 = r1 * (1.0 / (c1[j + 1 : j + 2, :] - ratio * c1[j : j + 1, :]))
        u0 = (r0 - c1[j : j + 1, :] * u1) * ia
        nxt = m - (c0 * jnp.broadcast_to(u0, (K, 128)) + c1 * jnp.broadcast_to(u1, (K, 128)))
        m = jnp.where(rows > j + 1, nxt, jnp.where(rows == j + 1, jnp.broadcast_to(r1, (K, 128)), m))
    diag = jnp.sum(jnp.where(rows == lanes, m, 0.0), axis=1, keepdims=True)
    linv = pltpu.roll(m, 128 - K, 1) * (1.0 / jnp.sqrt(diag))
    linv = linv[:, 0:K]
    for i in range(3):
        bas_ref[i] = jnp.dot(linv, img_in[i], preferred_element_type=F32, precision=HIGHEST)
        img_ref[i] = img_in[i]
    nm_ref[...] = nm_in[...]


def per_device(frames, mean_structure, atom_weight, subspace):
    x = jnp.transpose(frames, (1, 0, 2))
    s = jnp.transpose(subspace, (1, 0, 2))
    vm = pl.BlockSpec(memory_space=pltpu.VMEM)
    anyspec = pl.BlockSpec(memory_space=pl.ANY)
    dma = pltpu.SemaphoreType.DMA
    V = pltpu.VMEM
    scratch = [
        V((3, AL), F32), V((1, AL), F32), V((3, NF, AL), F32), V((3, K, AL), BF16), V((NB, 3, 2 * FP, BLK), BF16), V((NB, 3, FP, BLK), BF16),
        V((12, NF, 128), F32), V((NY, NF, 128), F32), V((NY, K, 128), F32), V((2, K, 128), F32), V((K, 128), F32),
        V((NB * NC, 1, 128), F32), V((K, 128), BF16),
        V((NX * NC * NY, 8, 128), F32), V((NZ, 8, 128), F32),
        V((8, 2, 64, BLK), BF16), V((8, NX // 2, 2, 64, BLK), BF16),
        V((4, 80, BLK), BF16), V((4, NZ // 2, 80, BLK), BF16),
        V((4, 32, BLK), BF16), V((4, NZ // 2, 32, BLK), BF16),
        V((4, 32, BLK), BF16), V((4, NX // 2, 32, BLK), BF16),
        V((NZ, 64, BLK), F32), V((2, 80, BLK), F32),
        V((4, 2, 64, BLK), F32), V((4, NZ // 2 - 1, 80, BLK), F32),
        dma, dma, dma((CHUNKS,)), dma,
        dma((NY - 1,)), dma((NY - 1,)), dma((NY - 1,)), dma((NY - 1,)),
        dma((NB * NC - 1,)), dma((NB * NC - 1,)),
        dma, dma, dma, dma,
        dma((NX * NC * NY - 1,)), dma((NX * NC * NY - 1,)), dma((NZ - 1,)), dma((NZ - 1,)),
        dma((8, NX // 2)), dma((8, NX // 2)), dma((4, NZ // 2)), dma((4, NZ // 2)),
        dma((4, NZ // 2)), dma((4, NZ // 2)), dma((4, NX // 2)), dma((4, NX // 2)),
    ]
    shapes = [(3, BLK), (3, K, BLK), (8, 128)]
    nm, img, gram = pl.pallas_call(
        kernel,
        out_shape=tuple(jax.ShapeDtypeStruct(d, F32) for d in shapes),
        in_specs=[anyspec] * 4,
        out_specs=(vm, vm, vm),
        scratch_shapes=scratch,
        compiler_params=pltpu.CompilerParams(
            collective_id=0, has_side_effects=True, vmem_limit_bytes=60 * 1024 * 1024
        ),
    )(x, mean_structure, atom_weight.reshape(1, AL), s)
    shapes = [(3, BLK), (3, K, BLK), (3, K, BLK)]
    nm, img, bas = pl.pallas_call(
        finish,
        out_shape=tuple(jax.ShapeDtypeStruct(d, F32) for d in shapes),
        in_specs=[vm, vm, vm],
        out_specs=(vm, vm, vm),
    )(nm, img, gram)
    return nm, jnp.transpose(img, (1, 0, 2)), jnp.transpose(bas, (1, 0, 2))


def solution(mesh):
    return jax.shard_map(
        per_device,
        mesh=mesh,
        in_specs=(P("frames", None, "atoms"), P(None, "atoms"), P("atoms"), P(None, None, "atoms")),
        out_specs=(
            P(None, ("atoms", "frames")),
            P(None, None, ("atoms", "frames")),
            P(None, None, ("atoms", "frames")),
        ),
        check_vma=False,
    )
```

```python
import jax
import jax.numpy as jnp
from jax import lax
from jax.experimental import pallas as pl
from jax.experimental.pallas import tpu as pltpu
from jax.sharding import PartitionSpec as P

ATOMS = 98304
FRAMES = 1536
NEWTON = 8
NX, NZ, NC, NY = 4, 8, 2, 4
NF = 24
FP = 32
K = 32
AL = ATOMS // NY
BLK = AL // (NX * NZ * NC)
NB = NX * NZ
CHUNKS = 8
CW = AL // CHUNKS
STEP = 512
UNROLL = 16
VLHS = False
F32 = jnp.float32
BF16 = jnp.bfloat16
MESH = pl.DeviceIdType.MESH
HIGHEST = lax.Precision.HIGHEST
PARTS = ((3, 4), (5, 2), (6, 1), (7, 0))
NT = (((1,), (1,)), ((), ()))


def steps_of(n, half, direction):
    return n // 2 if (direction == 1) == (half == 0) else n // 2 - 1


def newton(m):
    norm = m[0] * m[0]
    for e in m[1:]:
        norm = norm + e * e
    inv = 1.0 / jnp.sqrt(norm)
    x = [e * inv for e in m]
    for _ in range(NEWTON):
        x00, x01, x02, x10, x11, x12, x20, x21, x22 = x
        cof = [
            x11 * x22 - x12 * x21,
            x12 * x20 - x10 * x22,
            x10 * x21 - x11 * x20,
            x02 * x21 - x01 * x22,
            x00 * x22 - x02 * x20,
            x01 * x20 - x00 * x21,
            x01 * x12 - x02 * x11,
            x02 * x10 - x00 * x12,
            x00 * x11 - x01 * x10,
        ]
        det = x00 * cof[0] + x01 * cof[1] + x02 * cof[2]
        r = 1.0 / det
        x = [0.5 * (a + c * r) for a, c in zip(x, cof)]
    return x


def kernel(
    x_hbm, ms_hbm, w_hbm, s_hbm, nm_ref, img_ref, g_ref,
    ms_ref, w_ref, xv, sv, dall, dsend, rot, ex1, ex2, pp, gsq, pba, cpt, gx, gz,
    a1s, a1r, b1s, b1r, a2s, a2r, h4s, h4r, b2s, b2r, acca, accb, taf, tbf,
    msem, wsem, xsem, ssem, y1s, y1r, y2s, y2r, px_s, px_r, pp_s, pp_r, dx_s, dx_r,
    gx_s, gx_r, gz_s, gz_r, a1ss, a1rs, b1ss, b1rs, a2ss, a2rs, h4ss, h4rs, b2ss, b2rs,
):
    y = lax.axis_index("atoms")
    n = lax.axis_index("frames")
    px = n // (NZ * NC)
    pz = (n // NC) % NZ
    pc = n % NC

    def dev(dx=0, dz=0, dc=0, dy=0):
        tx = (px + (dx + NX)) % NX
        tz = (pz + (dz + NZ)) % NZ
        tc = (pc + dc) % NC
        return ((y + dy) % NY, (tx * NZ + tz) * NC + tc)

    y_peers = [dev(dy=j) for j in range(1, NY)]
    f_peers = [dev(dx=j // (NZ * NC), dz=(j // NC) % NZ, dc=j % NC) for j in range(1, NB * NC)]
    p_peers = [dev(dy=j // (NX * NC), dx=(j // NC) % NX, dc=j % NC) for j in range(1, NX * NC * NY)]
    greet = f_peers + [p_peers[j - 1] for j in range(NX * NC, NX * NC * NY)]
    z_peers = [dev(dz=j) for j in range(1, NZ)]
    partner = dev(dc=1)

    mload = pltpu.make_async_copy(ms_hbm, ms_ref, msem)
    wload = pltpu.make_async_copy(w_hbm, w_ref, wsem)
    wload.start()
    mload.start()
    loads = []
    for q in range(CHUNKS):
        cols = pl.ds(q * CW, CW)
        cp = pltpu.make_async_copy(x_hbm.at[:, :, cols], xv.at[:, :, cols], xsem.at[q])
        loads.append(cp)
    for cp in loads[:2]:
        cp.start()
    sload = pltpu.make_async_copy(s_hbm, sv, ssem)

    barrier = pltpu.get_barrier_semaphore()
    for peer in greet:
        pl.semaphore_signal(barrier, inc=1, device_id=peer, device_id_type=MESH)

    def remote(src, dst, ssm, rsm, peer):
        return pltpu.make_async_remote_copy(
            src_ref=src, dst_ref=dst, send_sem=ssm, recv_sem=rsm, device_id=peer, device_id_type=MESH
        )

    pending = []

    def exchange(buf, peers, ssm, rsm):
        copies = []
        for j, peer in enumerate(peers):
            copies.append(remote(buf.at[0], buf.at[j + 1], ssm.at[j], rsm.at[j], peer))
        for c in copies:
            c.start()
        for c in copies:
            c.wait_recv()
        pending.extend(copies)

    lane = lax.broadcasted_iota(jnp.int32, (NF, 128), 1)

    wload.wait()
    mload.wait()
    for cp in loads[2:]:
        cp.start()
    lc = jnp.sum(ms_ref[:, 0:2048], axis=1, keepdims=True) * (1.0 / 2048)

    def sums_body(q, acc):
        acc = list(acc)
        tw, tm = acc[12:]
        cols = pl.ds(pl.multiple_of(q * STEP, STEP), STEP)
        wv = w_ref[:, cols]
        wm = (ms_ref[:, cols] - lc) * wv
        acc[12:] = [tw + wv, tm + wm]
        for t in range(STEP // 128):
            lo = t * 128
            sub = pl.ds(pl.multiple_of(q * STEP + lo, 128), 128)
            wt = jnp.broadcast_to(wv[:, lo : lo + 128], (NF, 128))
            mt = [jnp.broadcast_to(wm[i : i + 1, lo : lo + 128], (NF, 128)) for i in range(3)]
            for j in range(3):
                xj = xv[j, :, sub]
                acc[j] = acc[j] + xj * wt
                for i in range(3):
                    acc[3 + i * 3 + j] = acc[3 + i * 3 + j] + xj * mt[i]
        return tuple(acc)

    acc = tuple(jnp.zeros((NF, 128), F32) for _ in range(12))
    acc += (jnp.zeros((1, STEP), F32), jnp.zeros((3, STEP), F32))
    per = CW // STEP
    for q in range(CHUNKS):
        if q == CHUNKS - 1:
            sload.start()
        loads[q].wait()
        acc = lax.fori_loop(q * per, (q + 1) * per, sums_body, acc)
    tw = jnp.sum(acc[12], axis=1, keepdims=True)
    tm = jnp.sum(acc[13], axis=1, keepdims=True) + lc * tw
    sums = [jnp.broadcast_to(jnp.sum(a, axis=1, keepdims=True), (NF, 128)) for a in acc[:12]]
    wide = [jnp.broadcast_to(lc[i : i + 1], (NF, 128)) for i in range(3)]
    wide_m = [jnp.broadcast_to(tm[i : i + 1], (NF, 128)) for i in range(3)]
    tile = jnp.broadcast_to(tw, (NF, 128))
    for i in range(3):
        for j in range(3):
            e = 3 * i + j
            tile = jnp.where(lane == e, sums[3 + e], tile)
            tile = jnp.where(lane == 16 + e, sums[j], tile)
            tile = jnp.where(lane == 32 + e, wide[i], tile)
            tile = jnp.where(lane == 48 + e, wide_m[i], tile)
    ex1[0] = tile
    pl.semaphore_wait(barrier, len(greet))
    exchange(ex1, y_peers, y1s, y1r)

    slots = [ex1[j] for j in range(NY)]
    tsum = slots[0] + slots[1] + slots[2] + slots[3]
    inv_total = 1.0 / jnp.broadcast_to(tsum[:, 127:128], (NF, 128))
    tsum = tsum * inv_total
    mrep = pltpu.roll(tsum, 128 - 48, 1)
    packed = None
    for p in slots:
        t = p + (pltpu.roll(p, 128 - 32, 1) - mrep) * pltpu.roll(p, 128 - 16, 1)
        packed = t if packed is None else packed + t
    packed = packed * inv_total
    r = newton([jnp.broadcast_to(packed[:, q : q + 1], (NF, 128)) for q in range(9)])
    fc = [jnp.broadcast_to(tsum[:, 16 + j : 17 + j], (NF, 128)) for j in range(3)]
    mc = [jnp.broadcast_to(tsum[:, 48 + 3 * i : 49 + 3 * i], (NF, 128)) for i in range(3)]
    for q in range(9):
        rot[q] = r[q]
    for i in range(3):
        off = r[3 * i] * fc[0] + r[3 * i + 1] * fc[1] + r[3 * i + 2] * fc[2]
        rot[9 + i] = mc[i] - off

    sload.wait()

    def move_body(own):
        def body(g, acc):
            core = pc if own else 1 - pc
            for i in range(3):
                vs, ss = [], []
                for u in range(UNROLL):
                    b = g * UNROLL + u
                    base = (b * NC + core) * BLK
                    pieces = []
                    for t in range(BLK // 128):
                        sub = pl.ds(pl.multiple_of(base + t * 128, 128), 128)
                        v = rot[3 * i] * xv[0, :, sub] + rot[3 * i + 1] * xv[1, :, sub] + rot[3 * i + 2] * xv[2, :, sub]
                        v = v + rot[9 + i] - jnp.broadcast_to(ms_ref[i : i + 1, sub], (NF, 128))
                        pieces.append(v)
                    v = jnp.concatenate(pieces, axis=1)
                    v = jnp.concatenate([v, jnp.zeros((FP - NF, BLK), F32)], axis=0).astype(BF16)
                    if own:
                        dall[b, i, 0:FP, :] = v
                    else:
                        dsend[b, i] = v
                    vs.append(v)
                    ss.append(sv[i, :, pl.ds(pl.multiple_of(base, 128), BLK)])
                vs = jnp.concatenate(vs, axis=1)
                ss = jnp.concatenate(ss, axis=1)
                if VLHS:
                    acc = acc + lax.dot_general(vs, ss, NT, preferred_element_type=F32)
                else:
                    acc = acc + lax.dot_general(ss, vs, NT, preferred_element_type=F32)
            return acc

        return body

    pacc = lax.fori_loop(0, NB // UNROLL, move_body(False), jnp.zeros((K, FP), F32))
    dcopy = remote(dsend, dall.at[:, :, FP : 2 * FP, :], dx_s, dx_r, partner)
    dcopy.start()
    pacc = lax.fori_loop(0, NB // UNROLL, move_body(True), pacc)
    if VLHS:
        pacc = pacc.T

    ex2[0] = jnp.zeros((K, 128), F32)
    ex2[0, :, 0:FP] = pacc
    exchange(ex2, y_peers, y2s, y2r)
    ptot = ex2[0] + ex2[1] + ex2[2] + ex2[3]
    pp[0] = ptot
    pcopy = remote(pp.at[0], pp.at[1], pp_s, pp_r, partner)
    pcopy.start()
    rows = lax.broadcasted_iota(jnp.int32, (K, 128), 0)
    lanes = lax.broadcasted_iota(jnp.int32, (K, 128), 1)
    col = jnp.broadcast_to(jnp.sum(ptot, axis=1, keepdims=True), (K, 128))
    row = jnp.sum(jnp.where(rows == lanes, col, 0.0), axis=0, keepdims=True)
    pba[0] = row
    exchange(pba, f_peers, px_s, px_r)
    row = jnp.broadcast_to(jnp.sum(pba[...], axis=0), (K, 128))
    pbar = jnp.sum(jnp.where(rows == lanes, row, 0.0), axis=1, keepdims=True) / FRAMES
    pcopy.wait_recv()
    other = pltpu.roll(pp[1], FP, 1)
    both = jnp.where(lanes < FP, ptot, other) - pbar
    cpt[...] = both.astype(BF16)
    dcopy.wait_recv()

    erow = lax.broadcasted_iota(jnp.int32, (16, 2 * FP), 0)
    ones = [jnp.where(erow == i, 1.0, 0.0).astype(BF16) for i in range(6)]
    coef = cpt[:, 0 : 2 * FP]
    coef2 = [jnp.concatenate([coef, ones[3 * q + 2]], axis=0) for q in range(2)]

    def mm(lhs, rhs):
        return jnp.dot(lhs, rhs, preferred_element_type=F32)

    def zblk(g, q):
        return (pz + PARTS[g][q]) % NZ

    def term_a(dest, g, emit):
        for q in range(2):
            blk = dest * NZ + zblk(g, q)
            for i in range(2):
                emit(q, i, mm(coef, dall[blk, i]))

    def term_b(dest, h, ref):
        tail = None
        for q in range(2):
            blk = (h * (NX // 2) + q) * NZ + dest
            t = mm(coef2[q], dall[blk, 2])
            ref[32 * q : 32 * q + 32, :] = t[0:32].astype(ref.dtype)
            t = t[32:48] + (mm(ones[3 * q], dall[blk, 0]) + mm(ones[3 * q + 1], dall[blk, 1]))
            tail = t if tail is None else tail + t
        ref[64:80, :] = tail.astype(ref.dtype)

    def rowslice(i):
        return slice(32 * i, 32 * i + 32)

    def store(ref, rows_of):
        def emit(q, i, t):
            ref[q, rows_of(i), :] = t.astype(ref.dtype)

        return emit

    class Stage:
        def __init__(self, length, pos, parts, sbuf, rbuf, ssm, rsm, fill, peer_of, subs):
            self.length, self.pos, self.sbuf, self.rbuf = length, pos, sbuf, rbuf
            self.ssm, self.rsm, self.fill, self.peer_of, self.subs = ssm, rsm, fill, peer_of, subs
            self.streams = tuple((h, d) for h in range(parts) for d in (1, -1))
            self.copies = {}
            self.filled = set()

        def steps(self, st):
            h, d = self.streams[st]
            return steps_of(self.length, h % 2, d)

        def dest(self, st, s):
            h, d = self.streams[st]
            return (self.pos + (d * (self.steps(st) - s) + self.length)) % self.length

        def prepare(self, st):
            self.fill(self.sbuf.at[st], st, 0, None)
            self.filled.add(st)

        def send(self, st, s):
            h, d = self.streams[st]
            if s >= self.steps(st):
                return
            if s == 0:
                src = self.sbuf.at[st]
                if st not in self.filled:
                    self.prepare(st)
            else:
                src = self.rbuf.at[st, s - 1]
            for k, sub in enumerate(self.subs):
                if s:
                    self.copies[st, s - 1, k].wait_recv()
                    self.fill(src.at[sub], st, s, sub)
                c = remote(
                    src.at[sub], self.rbuf.at[st, s].at[sub], self.ssm.at[st, s, k], self.rsm.at[st, s, k],
                    self.peer_of(d),
                )
                c.start()
                pending.append(c)
                self.copies[st, s, k] = c

        def finals(self, h):
            out = []
            for st, (hh, d) in enumerate(self.streams):
                if hh == h:
                    s = self.steps(st) - 1
                    for k in range(len(self.subs)):
                        self.copies[st, s, k].wait_recv()
                    out.append(self.rbuf.at[st, s])
            return out

    def fill_a1(ref, st, s, sub):
        g = st // 2
        if s == 0:
            term_a(sa1.dest(st, 0), g, store(ref, rowslice))
        else:
            ref[...] = (taf[g] + ref[...].astype(F32)).astype(BF16)

    def fill_b1(ref, st, s, sub):
        if s == 0:
            term_b(sb1.dest(st, 0), st // 2, ref)
        else:
            ref[...] = (tbf[st, s - 1, sub] + ref[...].astype(F32)).astype(BF16)

    x_dir = {1: dev(dx=1), -1: dev(dx=-1)}
    z_dir = {1: dev(dz=1), -1: dev(dz=-1)}
    sa1 = Stage(NX, px, 4, a1s, a1r, a1ss, a1rs, fill_a1, x_dir.get, (slice(0, 2),))
    sb1 = Stage(NZ, pz, 2, b1s, b1r, b1ss, b1rs, fill_b1, z_dir.get, (slice(0, 32), slice(32, 80)))

    order = (0, 3, 2, 1)
    for st in order:
        sa1.send(st, 0)
        sb1.send(st, 0)

    def terms_b(s):
        for st in order:
            if s < sb1.steps(st):
                term_b(sb1.dest(st, s), st // 2, tbf.at[st, s - 1])

    def terms_a(st):
        term_a(sa1.dest(st, 1), st // 2, store(taf.at[st // 2], rowslice))

    terms_a(0)
    terms_a(3)
    terms_b(1)
    for st in (4, 7, 6, 5):
        sa1.prepare(st)
    for st in (0, 3):
        sb1.send(st, 1)
        sa1.send(st, 1)
    for st in (4, 7, 6, 5):
        sa1.send(st, 0)
    for st in (2, 1):
        sb1.send(st, 1)
    terms_b(2)
    terms_b(3)
    terms_a(4)
    terms_a(7)

    def own_a(g):
        def emit(q, i, t):
            acca[zblk(g, q), rowslice(i), :] = t

        term_a(px, g, emit)

    def fin_a(g):
        f0, f1 = sa1.finals(g)
        for q in range(2):
            z = zblk(g, q)
            acca[z] = acca[z] + (f0[q].astype(F32) + f1[q].astype(F32))

    own_a(0)
    own_a(1)
    for st in order:
        sb1.send(st, 2)

    second = {}

    def straight(key, src, dst, ssm, rsm, peer):
        c = remote(src, dst, ssm, rsm, peer)
        c.start()
        pending.append(c)
        second[key] = c

    def send_z(r, merged=None):
        t = acca[(pz + r) % NZ]
        if merged is None:
            a2s[r] = t.astype(BF16)
        else:
            half = rowslice(merged)
            second["h", merged].wait_recv()
            a2s[r] = t.astype(BF16)
            a2s[r, half, :] = (acca[(pz + r) % NZ, half, :] + h4r[merged].astype(F32)).astype(BF16)
        straight(("z", r), a2s.at[r], a2r.at[r], a2ss.at[r], a2rs.at[r], z_peers[r - 1])

    fin_a(0)
    fin_a(1)
    for h, d in ((0, 1), (1, -1)):
        h4s[h] = acca[(pz + 4) % NZ, rowslice(h), :].astype(BF16)
        straight(("h", h), h4s.at[h], h4r.at[h], h4ss.at[h], h4rs.at[h], z_dir[d])
    send_z(2)
    own_a(2)
    own_a(3)
    for h in (0, 1):
        term_b(pz, h, accb.at[h])
    sa1.send(4, 1)
    sa1.send(7, 1)
    for st in order:
        sb1.send(st, 3)
    send_z(3, 0)
    send_z(5, 1)
    fin_a(2)
    fin_a(3)
    for r in (6, 1, 7):
        send_z(r)
    for h in (0, 1):
        f0, f1 = sb1.finals(h)
        accb[h] = accb[h] + (f0[...].astype(F32) + f1[...].astype(F32))

    def own_b(e):
        return accb[e // 2, pl.ds(pl.multiple_of(e % 2 * 32, 32), 32), :]

    for d in (2, 1, 3):
        e = (px + d) % NX
        b2s[d, 0:32, :] = own_b(e).astype(BF16)
        b2s[d, 32:48, :] = accb[e // 2, 64:80, :].astype(BF16)
        straight(("x", d), b2s.at[d], b2r.at[d], b2ss.at[d], b2rs.at[d], dev(dx=d))

    inv_f = 1.0 / FRAMES
    whole = acca[pz]
    for r in (2, 3, 5, 6, 1, 7):
        second["z", r].wait_recv()
        whole = whole + a2r[r].astype(F32)
    whole = whole * inv_f
    img2 = own_b(px)
    shift = accb[px // 2, 64:80, :]
    for d in (2, 1, 3):
        second["x", d].wait_recv()
        img2 = img2 + b2r[d, 0:32, :].astype(F32)
        shift = shift + b2r[d, 32:48, :].astype(F32)
    img2 = img2 * inv_f
    shift = jnp.where(px % 2 == 0, shift[0:3], shift[3:6])
    own = pl.ds(pl.multiple_of(n * BLK, 128), BLK)
    nm_ref[...] = ms_ref[:, own] + shift * inv_f
    imgs = [whole[0:32], whole[32:64]]
    imgs.append(img2)
    g = None
    for i in range(3):
        img_ref[i] = imgs[i]
        t = lax.dot_general(imgs[i], imgs[i], NT, preferred_element_type=F32, precision=HIGHEST)
        g = t if g is None else g + t
    gsq[...] = jnp.zeros((K, 128), F32)
    gsq[:, 0:K] = g
    v = gsq[0:8, :]
    for q in range(1, 4):
        v = v + pltpu.roll(gsq[8 * q : 8 * q + 8, :], 32 * q, 1)
    gx[0] = v
    exchange(gx, p_peers, gx_s, gx_r)
    gz[0] = jnp.sum(gx[...], axis=0)
    exchange(gz, z_peers, gz_s, gz_r)
    v = gz[0]
    for j in range(1, NZ):
        v = v + gz[j]
    g_ref[...] = v / (3 * ATOMS)

    for c in pending + [dcopy, pcopy]:
        c.wait_send()


def finish(nm_in, img_in, g_ref, nm_ref, img_ref, bas_ref):
    rows = lax.broadcasted_iota(jnp.int32, (K, 128), 0)
    lanes = lax.broadcasted_iota(jnp.int32, (K, 128), 1)
    v = g_ref[...]
    m = jnp.concatenate([v] + [pltpu.roll(v, 128 - 32 * q, 1) for q in range(1, 4)], axis=0)
    m = jnp.where(lanes < K, m, jnp.where(lanes - K == rows, 1.0, 0.0))
    for j in range(0, K, 2):
        r0 = m[j : j + 1, :]
        r1 = m[j + 1 : j + 2, :]
        c0 = jnp.broadcast_to(m[:, j : j + 1], (K, 128))
        c1 = jnp.broadcast_to(m[:, j + 1 : j + 2], (K, 128))
        ia = 1.0 / c0[j : j + 1, :]
        ratio = c0[j + 1 : j + 2, :] * ia
        r1 = r1 - ratio * r0
        u1 = r1 * (1.0 / (c1[j + 1 : j + 2, :] - ratio * c1[j : j + 1, :]))
        u0 = (r0 - c1[j : j + 1, :] * u1) * ia
        nxt = m - (c0 * jnp.broadcast_to(u0, (K, 128)) + c1 * jnp.broadcast_to(u1, (K, 128)))
        m = jnp.where(rows > j + 1, nxt, jnp.where(rows == j + 1, jnp.broadcast_to(r1, (K, 128)), m))
    diag = jnp.sum(jnp.where(rows == lanes, m, 0.0), axis=1, keepdims=True)
    linv = pltpu.roll(m, 128 - K, 1) * (1.0 / jnp.sqrt(diag))
    linv = linv[:, 0:K]
    for i in range(3):
        bas_ref[i] = jnp.dot(linv, img_in[i], preferred_element_type=F32, precision=HIGHEST)
        img_ref[i] = img_in[i]
    nm_ref[...] = nm_in[...]


def per_device(frames, mean_structure, atom_weight, subspace):
    x = jnp.transpose(frames, (1, 0, 2))
    s = jnp.transpose(subspace, (1, 0, 2))
    vm = pl.BlockSpec(memory_space=pltpu.VMEM)
    anyspec = pl.BlockSpec(memory_space=pl.ANY)
    dma = pltpu.SemaphoreType.DMA
    V = pltpu.VMEM
    scratch = [
        V((3, AL), F32), V((1, AL), F32), V((3, NF, AL), F32), V((3, K, AL), BF16), V((NB, 3, 2 * FP, BLK), BF16), V((NB, 3, FP, BLK), BF16),
        V((12, NF, 128), F32), V((NY, NF, 128), F32), V((NY, K, 128), F32), V((2, K, 128), F32), V((K, 128), F32),
        V((NB * NC, 1, 128), F32), V((K, 128), BF16),
        V((NX * NC * NY, 8, 128), F32), V((NZ, 8, 128), F32),
        V((8, 2, 64, BLK), BF16), V((8, NX // 2, 2, 64, BLK), BF16),
        V((4, 80, BLK), BF16), V((4, NZ // 2, 80, BLK), BF16),
        V((NZ, 64, BLK), BF16), V((NZ, 64, BLK), BF16), V((2, 32, BLK), BF16), V((2, 32, BLK), BF16),
        V((NX, 48, BLK), BF16), V((NX, 48, BLK), BF16),
        V((NZ, 64, BLK), F32), V((2, 80, BLK), F32),
        V((4, 2, 64, BLK), F32), V((4, NZ // 2 - 1, 80, BLK), F32),
        dma, dma, dma((CHUNKS,)), dma,
        dma((NY - 1,)), dma((NY - 1,)), dma((NY - 1,)), dma((NY - 1,)),
        dma((NB * NC - 1,)), dma((NB * NC - 1,)),
        dma, dma, dma, dma,
        dma((NX * NC * NY - 1,)), dma((NX * NC * NY - 1,)), dma((NZ - 1,)), dma((NZ - 1,)),
        dma((8, NX // 2, 1)), dma((8, NX // 2, 1)), dma((4, NZ // 2, 2)), dma((4, NZ // 2, 2)),
        dma((NZ,)), dma((NZ,)), dma((2,)), dma((2,)), dma((NX,)), dma((NX,)),
    ]
    shapes = [(3, BLK), (3, K, BLK), (8, 128)]
    nm, img, gram = pl.pallas_call(
        kernel,
        out_shape=tuple(jax.ShapeDtypeStruct(d, F32) for d in shapes),
        in_specs=[anyspec] * 4,
        out_specs=(vm, vm, vm),
        scratch_shapes=scratch,
        compiler_params=pltpu.CompilerParams(
            collective_id=0, has_side_effects=True, vmem_limit_bytes=60 * 1024 * 1024
        ),
    )(x, mean_structure, atom_weight.reshape(1, AL), s)
    shapes = [(3, BLK), (3, K, BLK), (3, K, BLK)]
    nm, img, bas = pl.pallas_call(
        finish,
        out_shape=tuple(jax.ShapeDtypeStruct(d, F32) for d in shapes),
        in_specs=[vm, vm, vm],
        out_specs=(vm, vm, vm),
    )(nm, img, gram)
    return nm, jnp.transpose(img, (1, 0, 2)), jnp.transpose(bas, (1, 0, 2))


def solution(mesh):
    return jax.shard_map(
        per_device,
        mesh=mesh,
        in_specs=(P("frames", None, "atoms"), P(None, "atoms"), P("atoms"), P(None, None, "atoms")),
        out_specs=(
            P(None, ("atoms", "frames")),
            P(None, None, ("atoms", "frames")),
            P(None, None, ("atoms", "frames")),
        ),
        check_vma=False,
    )
```

```python
import jax
import jax.numpy as jnp
from jax import lax
from jax.experimental import pallas as pl
from jax.experimental.pallas import tpu as pltpu
from jax.sharding import PartitionSpec as P

ATOMS = 98304
FRAMES = 1536
NEWTON = 8
NX, NZ, NC, NY = 4, 8, 2, 4
NF = 24
FP = 32
K = 32
AL = ATOMS // NY
BLK = AL // (NX * NZ * NC)
NB = NX * NZ
CHUNKS = 8
CW = AL // CHUNKS
STEP = 1024
UNROLL = 16
VLHS = False
F32 = jnp.float32
BF16 = jnp.bfloat16
MESH = pl.DeviceIdType.MESH
HIGHEST = lax.Precision.HIGHEST
PARTS = ((3, 4), (5, 2), (6, 1), (7, 0))
NT = (((1,), (1,)), ((), ()))


def steps_of(n, half, direction):
    return n // 2 if (direction == 1) == (half == 0) else n // 2 - 1


def newton(m):
    norm = m[0] * m[0]
    for e in m[1:]:
        norm = norm + e * e
    inv = 1.0 / jnp.sqrt(norm)
    x = [e * inv for e in m]
    for _ in range(NEWTON):
        x00, x01, x02, x10, x11, x12, x20, x21, x22 = x
        cof = [
            x11 * x22 - x12 * x21,
            x12 * x20 - x10 * x22,
            x10 * x21 - x11 * x20,
            x02 * x21 - x01 * x22,
            x00 * x22 - x02 * x20,
            x01 * x20 - x00 * x21,
            x01 * x12 - x02 * x11,
            x02 * x10 - x00 * x12,
            x00 * x11 - x01 * x10,
        ]
        det = x00 * cof[0] + x01 * cof[1] + x02 * cof[2]
        r = 1.0 / det
        x = [0.5 * (a + c * r) for a, c in zip(x, cof)]
    return x


def kernel(
    x_hbm, ms_hbm, w_hbm, s_hbm, nm_ref, img_ref, g_ref,
    ms_ref, w_ref, xv, sv, dall, dsend, rot, ex1, ex2, pp, gsq, pba, cpt, gx, gz,
    a1s, a1r, b1s, b1r, a2s, a2r, h4s, h4r, b2s, b2r, acca, accb, taf, tbf,
    msem, wsem, xsem, ssem, y1s, y1r, y2s, y2r, px_s, px_r, pp_s, pp_r, dx_s, dx_r,
    gx_s, gx_r, gz_s, gz_r, a1ss, a1rs, b1ss, b1rs, a2ss, a2rs, h4ss, h4rs, b2ss, b2rs,
):
    y = lax.axis_index("atoms")
    n = lax.axis_index("frames")
    px = n // (NZ * NC)
    pz = (n // NC) % NZ
    pc = n % NC

    def dev(dx=0, dz=0, dc=0, dy=0):
        tx = (px + (dx + NX)) % NX
        tz = (pz + (dz + NZ)) % NZ
        tc = (pc + dc) % NC
        return ((y + dy) % NY, (tx * NZ + tz) * NC + tc)

    y_peers = [dev(dy=j) for j in range(1, NY)]
    f_peers = [dev(dx=j // (NZ * NC), dz=(j // NC) % NZ, dc=j % NC) for j in range(1, NB * NC)]
    p_peers = [dev(dy=j // (NX * NC), dx=(j // NC) % NX, dc=j % NC) for j in range(1, NX * NC * NY)]
    greet = f_peers + [p_peers[j - 1] for j in range(NX * NC, NX * NC * NY)]
    z_peers = [dev(dz=j) for j in range(1, NZ)]
    partner = dev(dc=1)

    mload = pltpu.make_async_copy(ms_hbm, ms_ref, msem)
    wload = pltpu.make_async_copy(w_hbm, w_ref, wsem)
    wload.start()
    mload.start()
    loads = []
    for q in range(CHUNKS):
        cols = pl.ds(q * CW, CW)
        cp = pltpu.make_async_copy(x_hbm.at[:, :, cols], xv.at[:, :, cols], xsem.at[q])
        loads.append(cp)
    for cp in loads[:2]:
        cp.start()
    sload = pltpu.make_async_copy(s_hbm, sv, ssem)

    barrier = pltpu.get_barrier_semaphore()
    for peer in greet:
        pl.semaphore_signal(barrier, inc=1, device_id=peer, device_id_type=MESH)

    def remote(src, dst, ssm, rsm, peer):
        return pltpu.make_async_remote_copy(
            src_ref=src, dst_ref=dst, send_sem=ssm, recv_sem=rsm, device_id=peer, device_id_type=MESH
        )

    pending = []

    def exchange(buf, peers, ssm, rsm):
        copies = []
        for j, peer in enumerate(peers):
            copies.append(remote(buf.at[0], buf.at[j + 1], ssm.at[j], rsm.at[j], peer))
        for c in copies:
            c.start()
        for c in copies:
            c.wait_recv()
        pending.extend(copies)

    lane = lax.broadcasted_iota(jnp.int32, (NF, 128), 1)

    wload.wait()
    mload.wait()
    for cp in loads[2:]:
        cp.start()
    lc = jnp.sum(ms_ref[:, 0:2048], axis=1, keepdims=True) * (1.0 / 2048)

    def sums_body(q, acc):
        acc = list(acc)
        tw, tm = acc[12:]
        cols = pl.ds(pl.multiple_of(q * STEP, STEP), STEP)
        wv = w_ref[:, cols]
        wm = (ms_ref[:, cols] - lc) * wv
        acc[12:] = [tw + wv, tm + wm]
        for t in range(STEP // 128):
            lo = t * 128
            sub = pl.ds(pl.multiple_of(q * STEP + lo, 128), 128)
            wt = jnp.broadcast_to(wv[:, lo : lo + 128], (NF, 128))
            mt = [jnp.broadcast_to(wm[i : i + 1, lo : lo + 128], (NF, 128)) for i in range(3)]
            for j in range(3):
                xj = xv[j, :, sub]
                acc[j] = acc[j] + xj * wt
                for i in range(3):
                    acc[3 + i * 3 + j] = acc[3 + i * 3 + j] + xj * mt[i]
        return tuple(acc)

    acc = tuple(jnp.zeros((NF, 128), F32) for _ in range(12))
    acc += (jnp.zeros((1, STEP), F32), jnp.zeros((3, STEP), F32))
    per = CW // STEP
    for q in range(CHUNKS):
        if q == CHUNKS - 1:
            sload.start()
        loads[q].wait()
        acc = lax.fori_loop(q * per, (q + 1) * per, sums_body, acc)
    tw = jnp.sum(acc[12], axis=1, keepdims=True)
    tm = jnp.sum(acc[13], axis=1, keepdims=True) + lc * tw
    sums = [jnp.broadcast_to(jnp.sum(a, axis=1, keepdims=True), (NF, 128)) for a in acc[:12]]
    wide = [jnp.broadcast_to(lc[i : i + 1], (NF, 128)) for i in range(3)]
    wide_m = [jnp.broadcast_to(tm[i : i + 1], (NF, 128)) for i in range(3)]
    tile = jnp.broadcast_to(tw, (NF, 128))
    for i in range(3):
        for j in range(3):
            e = 3 * i + j
            tile = jnp.where(lane == e, sums[3 + e], tile)
            tile = jnp.where(lane == 9 + e, sums[j], tile)
            tile = jnp.where(lane == 18 + e, wide[i], tile)
            tile = jnp.where(lane == 27 + e, wide_m[i], tile)
    tile = jnp.where(lane < 42, tile, 0.0)
    ex1[0] = tile[0:8] + pltpu.roll(tile[8:16], 42, 1) + pltpu.roll(tile[16:24], 84, 1)
    pl.semaphore_wait(barrier, len(greet))
    exchange(ex1, y_peers, y1s, y1r)

    slots = []
    for j in range(NY):
        v = ex1[j]
        slots.append(jnp.concatenate([v, pltpu.roll(v, 128 - 42, 1), pltpu.roll(v, 128 - 84, 1)], axis=0))
    tsum = slots[0] + slots[1] + slots[2] + slots[3]
    inv_total = 1.0 / jnp.broadcast_to(tsum[:, 36:37], (NF, 128))
    tsum = tsum * inv_total
    mrep = pltpu.roll(tsum, 128 - 27, 1)
    packed = None
    for p in slots:
        t = p + (pltpu.roll(p, 128 - 18, 1) - mrep) * pltpu.roll(p, 128 - 9, 1)
        packed = t if packed is None else packed + t
    packed = packed * inv_total
    r = newton([jnp.broadcast_to(packed[:, q : q + 1], (NF, 128)) for q in range(9)])
    fc = [jnp.broadcast_to(tsum[:, 9 + j : 10 + j], (NF, 128)) for j in range(3)]
    mc = [jnp.broadcast_to(tsum[:, 27 + 3 * i : 28 + 3 * i], (NF, 128)) for i in range(3)]
    for q in range(9):
        rot[q] = r[q]
    for i in range(3):
        off = r[3 * i] * fc[0] + r[3 * i + 1] * fc[1] + r[3 * i + 2] * fc[2]
        rot[9 + i] = mc[i] - off

    sload.wait()

    def move_body(own):
        def body(g, acc):
            core = pc if own else 1 - pc
            for i in range(3):
                vs, ss = [], []
                for u in range(UNROLL):
                    b = g * UNROLL + u
                    base = (b * NC + core) * BLK
                    pieces = []
                    for t in range(BLK // 128):
                        sub = pl.ds(pl.multiple_of(base + t * 128, 128), 128)
                        v = rot[3 * i] * xv[0, :, sub] + rot[3 * i + 1] * xv[1, :, sub] + rot[3 * i + 2] * xv[2, :, sub]
                        v = v + rot[9 + i] - jnp.broadcast_to(ms_ref[i : i + 1, sub], (NF, 128))
                        pieces.append(v)
                    v = jnp.concatenate(pieces, axis=1)
                    v = jnp.concatenate([v, jnp.zeros((FP - NF, BLK), F32)], axis=0).astype(BF16)
                    if own:
                        dall[b, i, 0:FP, :] = v
                    else:
                        dsend[b, i] = v
                    vs.append(v)
                    ss.append(sv[i, :, pl.ds(pl.multiple_of(base, 128), BLK)])
                vs = jnp.concatenate(vs, axis=1)
                ss = jnp.concatenate(ss, axis=1)
                if VLHS:
                    acc = acc + lax.dot_general(vs, ss, NT, preferred_element_type=F32)
                else:
                    acc = acc + lax.dot_general(ss, vs, NT, preferred_element_type=F32)
            return acc

        return body

    pacc = lax.fori_loop(0, NB // UNROLL, move_body(False), jnp.zeros((K, FP), F32))
    dcopy = remote(dsend, dall.at[:, :, FP : 2 * FP, :], dx_s, dx_r, partner)
    dcopy.start()
    pacc = lax.fori_loop(0, NB // UNROLL, move_body(True), pacc)
    if VLHS:
        pacc = pacc.T

    rows = lax.broadcasted_iota(jnp.int32, (K, 128), 0)
    lanes = lax.broadcasted_iota(jnp.int32, (K, 128), 1)
    gsq[...] = jnp.zeros((K, 128), F32)
    gsq[:, 0:FP] = pacc
    v = gsq[0:8, :]
    for q in range(1, 4):
        v = v + pltpu.roll(gsq[8 * q : 8 * q + 8, :], 32 * q, 1)
    ex2[0] = v
    exchange(ex2, y_peers, y2s, y2r)
    v = ex2[0] + ex2[1] + ex2[2] + ex2[3]
    ptot = jnp.concatenate([v] + [pltpu.roll(v, 128 - 32 * q, 1) for q in range(1, 4)], axis=0)
    ptot = jnp.where(lanes < FP, ptot, 0.0)
    pp[0] = ptot
    pcopy = remote(pp.at[0], pp.at[1], pp_s, pp_r, partner)
    pcopy.start()
    col = jnp.broadcast_to(jnp.sum(ptot, axis=1, keepdims=True), (K, 128))
    row = jnp.sum(jnp.where(rows == lanes, col, 0.0), axis=0, keepdims=True)
    pba[0] = row
    exchange(pba, f_peers, px_s, px_r)
    row = jnp.broadcast_to(jnp.sum(pba[...], axis=0), (K, 128))
    pbar = jnp.sum(jnp.where(rows == lanes, row, 0.0), axis=1, keepdims=True) / FRAMES
    pcopy.wait_recv()
    other = pltpu.roll(pp[1], FP, 1)
    both = jnp.where(lanes < FP, ptot, other) - pbar
    cpt[...] = both.astype(BF16)
    dcopy.wait_recv()

    erow = lax.broadcasted_iota(jnp.int32, (16, 2 * FP), 0)
    ones = [jnp.where(erow == i, 1.0, 0.0).astype(BF16) for i in range(6)]
    coef = cpt[:, 0 : 2 * FP]
    coef2 = [jnp.concatenate([coef, ones[3 * q + 2]], axis=0) for q in range(2)]

    def mm(lhs, rhs):
        return jnp.dot(lhs, rhs, preferred_element_type=F32)

    def zblk(g, q):
        return (pz + PARTS[g][q]) % NZ

    def term_a(dest, g, emit):
        for q in range(2):
            blk = dest * NZ + zblk(g, q)
            for i in range(2):
                emit(q, i, mm(coef, dall[blk, i]))

    def term_b(dest, h, ref):
        tail = None
        for q in range(2):
            blk = (h * (NX // 2) + q) * NZ + dest
            t = mm(coef2[q], dall[blk, 2])
            ref[32 * q : 32 * q + 32, :] = t[0:32].astype(ref.dtype)
            t = t[32:48] + (mm(ones[3 * q], dall[blk, 0]) + mm(ones[3 * q + 1], dall[blk, 1]))
            tail = t if tail is None else tail + t
        ref[64:80, :] = tail.astype(ref.dtype)

    def rowslice(i):
        return slice(32 * i, 32 * i + 32)

    def store(ref, rows_of):
        def emit(q, i, t):
            ref[q, rows_of(i), :] = t.astype(ref.dtype)

        return emit

    class Stage:
        def __init__(self, length, pos, parts, sbuf, rbuf, ssm, rsm, fill, peer_of, subs):
            self.length, self.pos, self.sbuf, self.rbuf = length, pos, sbuf, rbuf
            self.ssm, self.rsm, self.fill, self.peer_of, self.subs = ssm, rsm, fill, peer_of, subs
            self.streams = tuple((h, d) for h in range(parts) for d in (1, -1))
            self.copies = {}
            self.filled = set()

        def steps(self, st):
            h, d = self.streams[st]
            return steps_of(self.length, h % 2, d)

        def dest(self, st, s):
            h, d = self.streams[st]
            return (self.pos + (d * (self.steps(st) - s) + self.length)) % self.length

        def prepare(self, st):
            self.fill(self.sbuf.at[st], st, 0, None)
            self.filled.add(st)

        def send(self, st, s):
            h, d = self.streams[st]
            if s >= self.steps(st):
                return
            if s == 0:
                src = self.sbuf.at[st]
                if st not in self.filled:
                    self.prepare(st)
            else:
                src = self.rbuf.at[st, s - 1]
            for k, sub in enumerate(self.subs):
                if s:
                    self.copies[st, s - 1, k].wait_recv()
                    self.fill(src.at[sub], st, s, sub)
                c = remote(
                    src.at[sub], self.rbuf.at[st, s].at[sub], self.ssm.at[st, s, k], self.rsm.at[st, s, k],
                    self.peer_of(d),
                )
                c.start()
                pending.append(c)
                self.copies[st, s, k] = c

        def finals(self, h):
            out = []
            for st, (hh, d) in enumerate(self.streams):
                if hh == h:
                    s = self.steps(st) - 1
                    for k in range(len(self.subs)):
                        self.copies[st, s, k].wait_recv()
                    out.append(self.rbuf.at[st, s])
            return out

    def fill_a1(ref, st, s, sub):
        g = st // 2
        if s == 0:
            term_a(sa1.dest(st, 0), g, store(ref, rowslice))
        else:
            ref[...] = (taf[g] + ref[...].astype(F32)).astype(BF16)

    def fill_b1(ref, st, s, sub):
        if s == 0:
            term_b(sb1.dest(st, 0), st // 2, ref)
        else:
            ref[...] = (tbf[st, s - 1, sub] + ref[...].astype(F32)).astype(BF16)

    x_dir = {1: dev(dx=1), -1: dev(dx=-1)}
    z_dir = {1: dev(dz=1), -1: dev(dz=-1)}
    sa1 = Stage(NX, px, 4, a1s, a1r, a1ss, a1rs, fill_a1, x_dir.get, (slice(0, 2),))
    sb1 = Stage(NZ, pz, 2, b1s, b1r, b1ss, b1rs, fill_b1, z_dir.get, (slice(0, 32), slice(32, 80)))

    order = (0, 3, 2, 1)
    for st in order:
        sa1.send(st, 0)
        sb1.send(st, 0)

    def terms_b(s):
        for st in order:
            if s < sb1.steps(st):
                term_b(sb1.dest(st, s), st // 2, tbf.at[st, s - 1])

    def terms_a(st):
        term_a(sa1.dest(st, 1), st // 2, store(taf.at[st // 2], rowslice))

    terms_a(0)
    terms_a(3)
    terms_b(1)
    for st in (4, 7, 6, 5):
        sa1.prepare(st)
    for st in (0, 3):
        sb1.send(st, 1)
        sa1.send(st, 1)
    for st in (4, 7, 6, 5):
        sa1.send(st, 0)
    for st in (2, 1):
        sb1.send(st, 1)
    terms_b(2)
    terms_b(3)
    terms_a(4)
    terms_a(7)

    def own_a(g):
        def emit(q, i, t):
            acca[zblk(g, q), rowslice(i), :] = t

        term_a(px, g, emit)

    def fin_a(g):
        f0, f1 = sa1.finals(g)
        for q in range(2):
            z = zblk(g, q)
            acca[z] = acca[z] + (f0[q].astype(F32) + f1[q].astype(F32))

    own_a(0)
    own_a(1)
    for st in order:
        sb1.send(st, 2)

    second = {}

    def straight(key, src, dst, ssm, rsm, peer):
        c = remote(src, dst, ssm, rsm, peer)
        c.start()
        pending.append(c)
        second[key] = c

    def send_z(r, merged=None):
        t = acca[(pz + r) % NZ]
        if merged is None:
            a2s[r] = t.astype(BF16)
        else:
            half = rowslice(merged)
            second["h", merged].wait_recv()
            a2s[r] = t.astype(BF16)
            a2s[r, half, :] = (acca[(pz + r) % NZ, half, :] + h4r[merged].astype(F32)).astype(BF16)
        straight(("z", r), a2s.at[r], a2r.at[r], a2ss.at[r], a2rs.at[r], z_peers[r - 1])

    fin_a(0)
    fin_a(1)
    for h, d in ((0, 1), (1, -1)):
        h4s[h] = acca[(pz + 4) % NZ, rowslice(h), :].astype(BF16)
        straight(("h", h), h4s.at[h], h4r.at[h], h4ss.at[h], h4rs.at[h], z_dir[d])
    own_a(2)
    own_a(3)
    for h in (0, 1):
        term_b(pz, h, accb.at[h])
    sa1.send(4, 1)
    sa1.send(7, 1)
    for st in order:
        sb1.send(st, 3)
    send_z(3, 0)
    send_z(5, 1)
    send_z(2)
    fin_a(2)
    fin_a(3)
    for r in (6, 1, 7):
        send_z(r)
    for h in (0, 1):
        f0, f1 = sb1.finals(h)
        accb[h] = accb[h] + (f0[...].astype(F32) + f1[...].astype(F32))

    def own_b(e):
        return accb[e // 2, pl.ds(pl.multiple_of(e % 2 * 32, 32), 32), :]

    for d in (2, 1, 3):
        e = (px + d) % NX
        b2s[d, 0:32, :] = own_b(e).astype(BF16)
        b2s[d, 32:48, :] = accb[e // 2, 64:80, :].astype(BF16)
        straight(("x", d), b2s.at[d], b2r.at[d], b2ss.at[d], b2rs.at[d], dev(dx=d))

    inv_f = 1.0 / FRAMES
    whole = acca[pz]
    for r in (2, 3, 5, 6, 1, 7):
        second["z", r].wait_recv()
        whole = whole + a2r[r].astype(F32)
    whole = whole * inv_f
    img2 = own_b(px)
    shift = accb[px // 2, 64:80, :]
    for d in (2, 1, 3):
        second["x", d].wait_recv()
        img2 = img2 + b2r[d, 0:32, :].astype(F32)
        shift = shift + b2r[d, 32:48, :].astype(F32)
    img2 = img2 * inv_f
    shift = jnp.where(px % 2 == 0, shift[0:3], shift[3:6])
    own = pl.ds(pl.multiple_of(n * BLK, 128), BLK)
    nm_ref[...] = ms_ref[:, own] + shift * inv_f
    imgs = [whole[0:32], whole[32:64]]
    imgs.append(img2)
    g = None
    for i in range(3):
        img_ref[i] = imgs[i]
        t = lax.dot_general(imgs[i], imgs[i], NT, preferred_element_type=F32, precision=HIGHEST)
        g = t if g is None else g + t
    gsq[...] = jnp.zeros((K, 128), F32)
    gsq[:, 0:K] = g
    v = gsq[0:8, :]
    for q in range(1, 4):
        v = v + pltpu.roll(gsq[8 * q : 8 * q + 8, :], 32 * q, 1)
    gx[0] = v
    exchange(gx, p_peers, gx_s, gx_r)
    gz[0] = jnp.sum(gx[...], axis=0)
    exchange(gz, z_peers, gz_s, gz_r)
    v = gz[0]
    for j in range(1, NZ):
        v = v + gz[j]
    g_ref[...] = v / (3 * ATOMS)

    for c in pending + [dcopy, pcopy]:
        c.wait_send()


def finish(nm_in, img_in, g_ref, nm_ref, img_ref, bas_ref):
    rows = lax.broadcasted_iota(jnp.int32, (K, 128), 0)
    lanes = lax.broadcasted_iota(jnp.int32, (K, 128), 1)
    v = g_ref[...]
    m = jnp.concatenate([v] + [pltpu.roll(v, 128 - 32 * q, 1) for q in range(1, 4)], axis=0)
    m = jnp.where(lanes < K, m, jnp.where(lanes - K == rows, 1.0, 0.0))
    for j in range(0, K, 2):
        r0 = m[j : j + 1, :]
        r1 = m[j + 1 : j + 2, :]
        c0 = jnp.broadcast_to(m[:, j : j + 1], (K, 128))
        c1 = jnp.broadcast_to(m[:, j + 1 : j + 2], (K, 128))
        ia = 1.0 / c0[j : j + 1, :]
        ratio = c0[j + 1 : j + 2, :] * ia
        r1 = r1 - ratio * r0
        u1 = r1 * (1.0 / (c1[j + 1 : j + 2, :] - ratio * c1[j : j + 1, :]))
        u0 = (r0 - c1[j : j + 1, :] * u1) * ia
        nxt = m - (c0 * jnp.broadcast_to(u0, (K, 128)) + c1 * jnp.broadcast_to(u1, (K, 128)))
        m = jnp.where(rows > j + 1, nxt, jnp.where(rows == j + 1, jnp.broadcast_to(r1, (K, 128)), m))
    diag = jnp.sum(jnp.where(rows == lanes, m, 0.0), axis=1, keepdims=True)
    linv = pltpu.roll(m, 128 - K, 1) * (1.0 / jnp.sqrt(diag))
    linv = linv[:, 0:K]
    for i in range(3):
        bas_ref[i] = jnp.dot(linv, img_in[i], preferred_element_type=F32, precision=HIGHEST)
        img_ref[i] = img_in[i]
    nm_ref[...] = nm_in[...]


def per_device(frames, mean_structure, atom_weight, subspace):
    x = jnp.transpose(frames, (1, 0, 2))
    s = jnp.transpose(subspace, (1, 0, 2))
    vm = pl.BlockSpec(memory_space=pltpu.VMEM)
    anyspec = pl.BlockSpec(memory_space=pl.ANY)
    dma = pltpu.SemaphoreType.DMA
    V = pltpu.VMEM
    scratch = [
        V((3, AL), F32), V((1, AL), F32), V((3, NF, AL), F32), V((3, K, AL), BF16), V((NB, 3, 2 * FP, BLK), BF16), V((NB, 3, FP, BLK), BF16),
        V((12, NF, 128), F32), V((NY, 8, 128), F32), V((NY, 8, 128), F32), V((2, K, 128), F32), V((K, 128), F32),
        V((NB * NC, 1, 128), F32), V((K, 128), BF16),
        V((NX * NC * NY, 8, 128), F32), V((NZ, 8, 128), F32),
        V((8, 2, 64, BLK), BF16), V((8, NX // 2, 2, 64, BLK), BF16),
        V((4, 80, BLK), BF16), V((4, NZ // 2, 80, BLK), BF16),
        V((NZ, 64, BLK), BF16), V((NZ, 64, BLK), BF16), V((2, 32, BLK), BF16), V((2, 32, BLK), BF16),
        V((NX, 48, BLK), BF16), V((NX, 48, BLK), BF16),
        V((NZ, 64, BLK), F32), V((2, 80, BLK), F32),
        V((4, 2, 64, BLK), F32), V((4, NZ // 2 - 1, 80, BLK), F32),
        dma, dma, dma((CHUNKS,)), dma,
        dma((NY - 1,)), dma((NY - 1,)), dma((NY - 1,)), dma((NY - 1,)),
        dma((NB * NC - 1,)), dma((NB * NC - 1,)),
        dma, dma, dma, dma,
        dma((NX * NC * NY - 1,)), dma((NX * NC * NY - 1,)), dma((NZ - 1,)), dma((NZ - 1,)),
        dma((8, NX // 2, 1)), dma((8, NX // 2, 1)), dma((4, NZ // 2, 2)), dma((4, NZ // 2, 2)),
        dma((NZ,)), dma((NZ,)), dma((2,)), dma((2,)), dma((NX,)), dma((NX,)),
    ]
    shapes = [(3, BLK), (3, K, BLK), (8, 128)]
    nm, img, gram = pl.pallas_call(
        kernel,
        out_shape=tuple(jax.ShapeDtypeStruct(d, F32) for d in shapes),
        in_specs=[anyspec] * 4,
        out_specs=(vm, vm, vm),
        scratch_shapes=scratch,
        compiler_params=pltpu.CompilerParams(
            collective_id=0, has_side_effects=True, vmem_limit_bytes=60 * 1024 * 1024
        ),
    )(x, mean_structure, atom_weight.reshape(1, AL), s)
    shapes = [(3, BLK), (3, K, BLK), (3, K, BLK)]
    nm, img, bas = pl.pallas_call(
        finish,
        out_shape=tuple(jax.ShapeDtypeStruct(d, F32) for d in shapes),
        in_specs=[vm, vm, vm],
        out_specs=(vm, vm, vm),
    )(nm, img, gram)
    return nm, jnp.transpose(img, (1, 0, 2)), jnp.transpose(bas, (1, 0, 2))


def solution(mesh):
    return jax.shard_map(
        per_device,
        mesh=mesh,
        in_specs=(P("frames", None, "atoms"), P(None, "atoms"), P("atoms"), P(None, None, "atoms")),
        out_specs=(
            P(None, ("atoms", "frames")),
            P(None, None, ("atoms", "frames")),
            P(None, None, ("atoms", "frames")),
        ),
        check_vma=False,
    )
```

```python
import jax
import jax.numpy as jnp
from jax import lax
from jax.experimental import pallas as pl
from jax.experimental.pallas import tpu as pltpu
from jax.sharding import PartitionSpec as P

ATOMS = 98304
FRAMES = 1536
NEWTON = 8
NX, NZ, NC, NY = 4, 8, 2, 4
NF = 24
FP = 32
K = 32
AL = ATOMS // NY
BLK = AL // (NX * NZ * NC)
NB = NX * NZ
CHUNKS = 8
CW = AL // CHUNKS
STEP = 1024
UNROLL = 16
VLHS = False
F32 = jnp.float32
BF16 = jnp.bfloat16
MESH = pl.DeviceIdType.MESH
HIGHEST = lax.Precision.HIGHEST
PARTS = ((3, 4), (5, 2), (6, 1), (7, 0))
NT = (((1,), (1,)), ((), ()))


def steps_of(n, half, direction):
    return n // 2 if (direction == 1) == (half == 0) else n // 2 - 1


def newton(m):
    norm = m[0] * m[0]
    for e in m[1:]:
        norm = norm + e * e
    inv = 1.0 / jnp.sqrt(norm)
    x = [e * inv for e in m]
    for _ in range(NEWTON):
        x00, x01, x02, x10, x11, x12, x20, x21, x22 = x
        cof = [
            x11 * x22 - x12 * x21,
            x12 * x20 - x10 * x22,
            x10 * x21 - x11 * x20,
            x02 * x21 - x01 * x22,
            x00 * x22 - x02 * x20,
            x01 * x20 - x00 * x21,
            x01 * x12 - x02 * x11,
            x02 * x10 - x00 * x12,
            x00 * x11 - x01 * x10,
        ]
        det = x00 * cof[0] + x01 * cof[1] + x02 * cof[2]
        r = 1.0 / det
        x = [0.5 * (a + c * r) for a, c in zip(x, cof)]
    return x


def kernel(
    x_hbm, ms_hbm, w_hbm, s_hbm, nm_ref, img_ref, g_ref,
    ms_ref, w_ref, xv, sv, dall, dsend, rot, ex1, ex2, pp, gsq, pba, cpt, gx, gz,
    a1s, a1r, b1s, b1r, a2s, a2r, h4s, h4r, b2s, b2r, acca, accb, taf, tbf,
    msem, wsem, xsem, ssem, y1s, y1r, y2s, y2r, px_s, px_r, pp_s, pp_r, dx_s, dx_r,
    gx_s, gx_r, gz_s, gz_r, a1ss, a1rs, b1ss, b1rs, a2ss, a2rs, h4ss, h4rs, b2ss, b2rs,
):
    y = lax.axis_index("atoms")
    n = lax.axis_index("frames")
    px = n // (NZ * NC)
    pz = (n // NC) % NZ
    pc = n % NC

    def dev(dx=0, dz=0, dc=0, dy=0):
        tx = (px + (dx + NX)) % NX
        tz = (pz + (dz + NZ)) % NZ
        tc = (pc + dc) % NC
        return ((y + dy) % NY, (tx * NZ + tz) * NC + tc)

    def hops(o):
        return sum(min(k, size - k) for k, size in zip(o, (NX, NY, NZ)))

    def peers(nx, ny, nz, nc):
        offsets = [
            (a, b, c, e) for a in range(nx) for b in range(ny) for c in range(nz) for e in range(nc) if a + b + c + e
        ]
        offsets.sort(key=lambda o: -hops(o))
        return [dev(dx=a, dy=b, dz=c, dc=e) for a, b, c, e in offsets]

    y_peers = peers(1, NY, 1, 1)
    f_peers = peers(NX, 1, NZ, NC)
    p_peers = peers(NX, NY, 1, NC)
    z_far = peers(1, 1, NZ, 1)
    greet = f_peers + [dev(dx=a, dy=b, dc=e) for a in range(NX) for b in range(1, NY) for e in range(NC)]
    z_peers = [dev(dz=j) for j in range(1, NZ)]
    partner = dev(dc=1)

    mload = pltpu.make_async_copy(ms_hbm, ms_ref, msem)
    wload = pltpu.make_async_copy(w_hbm, w_ref, wsem)
    wload.start()
    mload.start()
    loads = []
    for q in range(CHUNKS):
        cols = pl.ds(q * CW, CW)
        cp = pltpu.make_async_copy(x_hbm.at[:, :, cols], xv.at[:, :, cols], xsem.at[q])
        loads.append(cp)
    for cp in loads[:2]:
        cp.start()
    sload = pltpu.make_async_copy(s_hbm, sv, ssem)

    barrier = pltpu.get_barrier_semaphore()
    for peer in greet:
        pl.semaphore_signal(barrier, inc=1, device_id=peer, device_id_type=MESH)

    def remote(src, dst, ssm, rsm, peer):
        return pltpu.make_async_remote_copy(
            src_ref=src, dst_ref=dst, send_sem=ssm, recv_sem=rsm, device_id=peer, device_id_type=MESH
        )

    pending = []

    def exchange(buf, peers, ssm, rsm):
        copies = []
        for j, peer in enumerate(peers):
            copies.append(remote(buf.at[0], buf.at[j + 1], ssm.at[j], rsm.at[j], peer))
        for c in copies:
            c.start()
        for c in copies:
            c.wait_recv()
        pending.extend(copies)

    lane = lax.broadcasted_iota(jnp.int32, (NF, 128), 1)

    wload.wait()
    mload.wait()
    for cp in loads[2:]:
        cp.start()
    lc = jnp.sum(ms_ref[:, 0:2048], axis=1, keepdims=True) * (1.0 / 2048)

    def sums_body(q, acc):
        acc = list(acc)
        tw, tm = acc[12:]
        cols = pl.ds(pl.multiple_of(q * STEP, STEP), STEP)
        wv = w_ref[:, cols]
        wm = (ms_ref[:, cols] - lc) * wv
        acc[12:] = [tw + wv, tm + wm]
        for t in range(STEP // 128):
            lo = t * 128
            sub = pl.ds(pl.multiple_of(q * STEP + lo, 128), 128)
            wt = jnp.broadcast_to(wv[:, lo : lo + 128], (NF, 128))
            mt = [jnp.broadcast_to(wm[i : i + 1, lo : lo + 128], (NF, 128)) for i in range(3)]
            for j in range(3):
                xj = xv[j, :, sub]
                acc[j] = acc[j] + xj * wt
                for i in range(3):
                    acc[3 + i * 3 + j] = acc[3 + i * 3 + j] + xj * mt[i]
        return tuple(acc)

    acc = tuple(jnp.zeros((NF, 128), F32) for _ in range(12))
    acc += (jnp.zeros((1, STEP), F32), jnp.zeros((3, STEP), F32))
    per = CW // STEP
    for q in range(CHUNKS):
        if q == CHUNKS - 1:
            sload.start()
        loads[q].wait()
        acc = lax.fori_loop(q * per, (q + 1) * per, sums_body, acc)
    tw = jnp.sum(acc[12], axis=1, keepdims=True)
    tm = jnp.sum(acc[13], axis=1, keepdims=True) + lc * tw
    sums = [jnp.broadcast_to(jnp.sum(a, axis=1, keepdims=True), (NF, 128)) for a in acc[:12]]
    wide = [jnp.broadcast_to(lc[i : i + 1], (NF, 128)) for i in range(3)]
    wide_m = [jnp.broadcast_to(tm[i : i + 1], (NF, 128)) for i in range(3)]
    tile = jnp.broadcast_to(tw, (NF, 128))
    for i in range(3):
        for j in range(3):
            e = 3 * i + j
            tile = jnp.where(lane == e, sums[3 + e], tile)
            tile = jnp.where(lane == 9 + e, sums[j], tile)
            tile = jnp.where(lane == 18 + e, wide[i], tile)
            tile = jnp.where(lane == 27 + e, wide_m[i], tile)
    tile = jnp.where(lane < 42, tile, 0.0)
    ex1[0] = tile[0:8] + pltpu.roll(tile[8:16], 42, 1) + pltpu.roll(tile[16:24], 84, 1)
    pl.semaphore_wait(barrier, len(greet))
    exchange(ex1, y_peers, y1s, y1r)

    slots = []
    for j in range(NY):
        v = ex1[j]
        slots.append(jnp.concatenate([v, pltpu.roll(v, 128 - 42, 1), pltpu.roll(v, 128 - 84, 1)], axis=0))
    tsum = slots[0] + slots[1] + slots[2] + slots[3]
    inv_total = 1.0 / jnp.broadcast_to(tsum[:, 36:37], (NF, 128))
    tsum = tsum * inv_total
    mrep = pltpu.roll(tsum, 128 - 27, 1)
    packed = None
    for p in slots:
        t = p + (pltpu.roll(p, 128 - 18, 1) - mrep) * pltpu.roll(p, 128 - 9, 1)
        packed = t if packed is None else packed + t
    packed = packed * inv_total
    r = newton([jnp.broadcast_to(packed[:, q : q + 1], (NF, 128)) for q in range(9)])
    fc = [jnp.broadcast_to(tsum[:, 9 + j : 10 + j], (NF, 128)) for j in range(3)]
    mc = [jnp.broadcast_to(tsum[:, 27 + 3 * i : 28 + 3 * i], (NF, 128)) for i in range(3)]
    for q in range(9):
        rot[q] = r[q]
    for i in range(3):
        off = r[3 * i] * fc[0] + r[3 * i + 1] * fc[1] + r[3 * i + 2] * fc[2]
        rot[9 + i] = mc[i] - off

    sload.wait()

    def move_body(own):
        def body(g, acc):
            core = pc if own else 1 - pc
            for i in range(3):
                vs, ss = [], []
                for u in range(UNROLL):
                    b = g * UNROLL + u
                    base = (b * NC + core) * BLK
                    pieces = []
                    for t in range(BLK // 128):
                        sub = pl.ds(pl.multiple_of(base + t * 128, 128), 128)
                        v = rot[3 * i] * xv[0, :, sub] + rot[3 * i + 1] * xv[1, :, sub] + rot[3 * i + 2] * xv[2, :, sub]
                        v = v + rot[9 + i] - jnp.broadcast_to(ms_ref[i : i + 1, sub], (NF, 128))
                        pieces.append(v)
                    v = jnp.concatenate(pieces, axis=1)
                    v = jnp.concatenate([v, jnp.zeros((FP - NF, BLK), F32)], axis=0).astype(BF16)
                    if own:
                        dall[b, i, 0:FP, :] = v
                    else:
                        dsend[b, i] = v
                    vs.append(v)
                    ss.append(sv[i, :, pl.ds(pl.multiple_of(base, 128), BLK)])
                vs = jnp.concatenate(vs, axis=1)
                ss = jnp.concatenate(ss, axis=1)
                if VLHS:
                    acc = acc + lax.dot_general(vs, ss, NT, preferred_element_type=F32)
                else:
                    acc = acc + lax.dot_general(ss, vs, NT, preferred_element_type=F32)
            return acc

        return body

    pacc = lax.fori_loop(0, NB // UNROLL, move_body(False), jnp.zeros((K, FP), F32))
    dcopy = remote(dsend, dall.at[:, :, FP : 2 * FP, :], dx_s, dx_r, partner)
    dcopy.start()
    pacc = lax.fori_loop(0, NB // UNROLL, move_body(True), pacc)
    if VLHS:
        pacc = pacc.T

    rows = lax.broadcasted_iota(jnp.int32, (K, 128), 0)
    lanes = lax.broadcasted_iota(jnp.int32, (K, 128), 1)
    gsq[...] = jnp.zeros((K, 128), F32)
    gsq[:, 0:FP] = pacc
    v = gsq[0:8, :]
    for q in range(1, 4):
        v = v + pltpu.roll(gsq[8 * q : 8 * q + 8, :], 32 * q, 1)
    ex2[0] = v
    exchange(ex2, y_peers, y2s, y2r)
    v = ex2[0] + ex2[1] + ex2[2] + ex2[3]
    ptot = jnp.concatenate([v] + [pltpu.roll(v, 128 - 32 * q, 1) for q in range(1, 4)], axis=0)
    ptot = jnp.where(lanes < FP, ptot, 0.0)
    pp[0] = ptot
    pcopy = remote(pp.at[0], pp.at[1], pp_s, pp_r, partner)
    pcopy.start()
    col = jnp.broadcast_to(jnp.sum(ptot, axis=1, keepdims=True), (K, 128))
    row = jnp.sum(jnp.where(rows == lanes, col, 0.0), axis=0, keepdims=True)
    pba[0] = row
    exchange(pba, f_peers, px_s, px_r)
    row = jnp.broadcast_to(jnp.sum(pba[...], axis=0), (K, 128))
    pbar = jnp.sum(jnp.where(rows == lanes, row, 0.0), axis=1, keepdims=True) / FRAMES
    pcopy.wait_recv()
    other = pltpu.roll(pp[1], FP, 1)
    both = jnp.where(lanes < FP, ptot, other) - pbar
    cpt[...] = both.astype(BF16)
    dcopy.wait_recv()

    erow = lax.broadcasted_iota(jnp.int32, (16, 2 * FP), 0)
    ones = [jnp.where(erow == i, 1.0, 0.0).astype(BF16) for i in range(6)]
    coef = cpt[:, 0 : 2 * FP]
    coef2 = [jnp.concatenate([coef, ones[3 * q + 2]], axis=0) for q in range(2)]

    def mm(lhs, rhs):
        return jnp.dot(lhs, rhs, preferred_element_type=F32)

    def zblk(g, q):
        return (pz + PARTS[g][q]) % NZ

    def term_a(dest, g, emit):
        for q in range(2):
            blk = dest * NZ + zblk(g, q)
            for i in range(2):
                emit(q, i, mm(coef, dall[blk, i]))

    def term_b(dest, h, ref):
        tail = None
        for q in range(2):
            blk = (h * (NX // 2) + q) * NZ + dest
            t = mm(coef2[q], dall[blk, 2])
            ref[32 * q : 32 * q + 32, :] = t[0:32].astype(ref.dtype)
            t = t[32:48] + (mm(ones[3 * q], dall[blk, 0]) + mm(ones[3 * q + 1], dall[blk, 1]))
            tail = t if tail is None else tail + t
        ref[64:80, :] = tail.astype(ref.dtype)

    def rowslice(i):
        return slice(32 * i, 32 * i + 32)

    def store(ref, rows_of):
        def emit(q, i, t):
            ref[q, rows_of(i), :] = t.astype(ref.dtype)

        return emit

    class Stage:
        def __init__(self, length, pos, parts, sbuf, rbuf, ssm, rsm, fill, peer_of, subs):
            self.length, self.pos, self.sbuf, self.rbuf = length, pos, sbuf, rbuf
            self.ssm, self.rsm, self.fill, self.peer_of, self.subs = ssm, rsm, fill, peer_of, subs
            self.streams = tuple((h, d) for h in range(parts) for d in (1, -1))
            self.copies = {}
            self.filled = set()

        def steps(self, st):
            h, d = self.streams[st]
            return steps_of(self.length, h % 2, d)

        def dest(self, st, s):
            h, d = self.streams[st]
            return (self.pos + (d * (self.steps(st) - s) + self.length)) % self.length

        def prepare(self, st):
            self.fill(self.sbuf.at[st], st, 0, None)
            self.filled.add(st)

        def send(self, st, s):
            h, d = self.streams[st]
            if s >= self.steps(st):
                return
            if s == 0:
                src = self.sbuf.at[st]
                if st not in self.filled:
                    self.prepare(st)
            else:
                src = self.rbuf.at[st, s - 1]
            for k, sub in enumerate(self.subs):
                if s:
                    self.copies[st, s - 1, k].wait_recv()
                    self.fill(src.at[sub], st, s, sub)
                c = remote(
                    src.at[sub], self.rbuf.at[st, s].at[sub], self.ssm.at[st, s, k], self.rsm.at[st, s, k],
                    self.peer_of(d),
                )
                c.start()
                pending.append(c)
                self.copies[st, s, k] = c

        def finals(self, h):
            out = []
            for st, (hh, d) in enumerate(self.streams):
                if hh == h:
                    s = self.steps(st) - 1
                    for k in range(len(self.subs)):
                        self.copies[st, s, k].wait_recv()
                    out.append(self.rbuf.at[st, s])
            return out

    def fill_a1(ref, st, s, sub):
        g = st // 2
        if s == 0:
            term_a(sa1.dest(st, 0), g, store(ref, rowslice))
        else:
            ref[...] = (taf[g] + ref[...].astype(F32)).astype(BF16)

    def fill_b1(ref, st, s, sub):
        if s == 0:
            term_b(sb1.dest(st, 0), st // 2, ref)
        else:
            ref[...] = (tbf[st, s - 1, sub] + ref[...].astype(F32)).astype(BF16)

    x_dir = {1: dev(dx=1), -1: dev(dx=-1)}
    z_dir = {1: dev(dz=1), -1: dev(dz=-1)}
    sa1 = Stage(NX, px, 4, a1s, a1r, a1ss, a1rs, fill_a1, x_dir.get, (slice(0, 2),))
    sb1 = Stage(NZ, pz, 2, b1s, b1r, b1ss, b1rs, fill_b1, z_dir.get, (slice(0, 32), slice(32, 80)))

    order = (0, 3, 2, 1)
    for st in order:
        sa1.send(st, 0)
        sb1.send(st, 0)

    def terms_b(s):
        for st in order:
            if s < sb1.steps(st):
                term_b(sb1.dest(st, s), st // 2, tbf.at[st, s - 1])

    def terms_a(st):
        term_a(sa1.dest(st, 1), st // 2, store(taf.at[st // 2], rowslice))

    terms_a(0)
    terms_a(3)
    terms_b(1)
    for st in (4, 7, 6, 5):
        sa1.prepare(st)
    for st in (0, 3):
        sb1.send(st, 1)
        sa1.send(st, 1)
    for st in (4, 7, 6, 5):
        sa1.send(st, 0)
    for st in (2, 1):
        sb1.send(st, 1)
    terms_b(2)
    terms_b(3)
    terms_a(4)
    terms_a(7)

    def own_a(g):
        def emit(q, i, t):
            acca[zblk(g, q), rowslice(i), :] = t

        term_a(px, g, emit)

    def fin_a(g):
        f0, f1 = sa1.finals(g)
        for q in range(2):
            z = zblk(g, q)
            acca[z] = acca[z] + (f0[q].astype(F32) + f1[q].astype(F32))

    own_a(0)
    own_a(1)
    for st in order:
        sb1.send(st, 2)

    second = {}

    def straight(key, src, dst, ssm, rsm, peer):
        c = remote(src, dst, ssm, rsm, peer)
        c.start()
        pending.append(c)
        second[key] = c

    def send_z(r, merged=None):
        t = acca[(pz + r) % NZ]
        if merged is None:
            a2s[r] = t.astype(BF16)
        else:
            half = rowslice(merged)
            second["h", merged].wait_recv()
            a2s[r] = t.astype(BF16)
            a2s[r, half, :] = (acca[(pz + r) % NZ, half, :] + h4r[merged].astype(F32)).astype(BF16)
        straight(("z", r), a2s.at[r], a2r.at[r], a2ss.at[r], a2rs.at[r], z_peers[r - 1])

    fin_a(0)
    fin_a(1)
    for h, d in ((0, 1), (1, -1)):
        h4s[h] = acca[(pz + 4) % NZ, rowslice(h), :].astype(BF16)
        straight(("h", h), h4s.at[h], h4r.at[h], h4ss.at[h], h4rs.at[h], z_dir[d])
    own_a(2)
    own_a(3)
    for h in (0, 1):
        term_b(pz, h, accb.at[h])
    sa1.send(4, 1)
    sa1.send(7, 1)
    for st in order:
        sb1.send(st, 3)
    send_z(3, 0)
    send_z(5, 1)
    send_z(2)
    fin_a(2)
    fin_a(3)
    for r in (6, 1, 7):
        send_z(r)
    for h in (0, 1):
        f0, f1 = sb1.finals(h)
        accb[h] = accb[h] + (f0[...].astype(F32) + f1[...].astype(F32))

    def own_b(e):
        return accb[e // 2, pl.ds(pl.multiple_of(e % 2 * 32, 32), 32), :]

    for d in (2, 1, 3):
        e = (px + d) % NX
        b2s[d, 0:32, :] = own_b(e).astype(BF16)
        b2s[d, 32:48, :] = accb[e // 2, 64:80, :].astype(BF16)
        straight(("x", d), b2s.at[d], b2r.at[d], b2ss.at[d], b2rs.at[d], dev(dx=d))

    inv_f = 1.0 / FRAMES
    whole = acca[pz]
    for r in (2, 3, 5, 6, 1, 7):
        second["z", r].wait_recv()
        whole = whole + a2r[r].astype(F32)
    whole = whole * inv_f
    img2 = own_b(px)
    shift = accb[px // 2, 64:80, :]
    for d in (2, 1, 3):
        second["x", d].wait_recv()
        img2 = img2 + b2r[d, 0:32, :].astype(F32)
        shift = shift + b2r[d, 32:48, :].astype(F32)
    img2 = img2 * inv_f
    shift = jnp.where(px % 2 == 0, shift[0:3], shift[3:6])
    own = pl.ds(pl.multiple_of(n * BLK, 128), BLK)
    nm_ref[...] = ms_ref[:, own] + shift * inv_f
    imgs = [whole[0:32], whole[32:64]]
    imgs.append(img2)
    g = None
    for i in range(3):
        img_ref[i] = imgs[i]
        t = lax.dot_general(imgs[i], imgs[i], NT, preferred_element_type=F32, precision=HIGHEST)
        g = t if g is None else g + t
    gsq[...] = jnp.zeros((K, 128), F32)
    gsq[:, 0:K] = g
    v = gsq[0:8, :]
    for q in range(1, 4):
        v = v + pltpu.roll(gsq[8 * q : 8 * q + 8, :], 32 * q, 1)
    gx[0] = v
    exchange(gx, p_peers, gx_s, gx_r)
    gz[0] = jnp.sum(gx[...], axis=0)
    exchange(gz, z_far, gz_s, gz_r)
    v = gz[0]
    for j in range(1, NZ):
        v = v + gz[j]
    g_ref[...] = v / (3 * ATOMS)

    for c in pending + [dcopy, pcopy]:
        c.wait_send()


def finish(nm_in, img_in, g_ref, nm_ref, img_ref, bas_ref):
    rows = lax.broadcasted_iota(jnp.int32, (K, 128), 0)
    lanes = lax.broadcasted_iota(jnp.int32, (K, 128), 1)
    v = g_ref[...]
    m = jnp.concatenate([v] + [pltpu.roll(v, 128 - 32 * q, 1) for q in range(1, 4)], axis=0)
    m = jnp.where(lanes < K, m, jnp.where(lanes - K == rows, 1.0, 0.0))
    for j in range(0, K, 2):
        r0 = m[j : j + 1, :]
        r1 = m[j + 1 : j + 2, :]
        c0 = jnp.broadcast_to(m[:, j : j + 1], (K, 128))
        c1 = jnp.broadcast_to(m[:, j + 1 : j + 2], (K, 128))
        ia = 1.0 / c0[j : j + 1, :]
        ratio = c0[j + 1 : j + 2, :] * ia
        r1 = r1 - ratio * r0
        u1 = r1 * (1.0 / (c1[j + 1 : j + 2, :] - ratio * c1[j : j + 1, :]))
        u0 = (r0 - c1[j : j + 1, :] * u1) * ia
        nxt = m - (c0 * jnp.broadcast_to(u0, (K, 128)) + c1 * jnp.broadcast_to(u1, (K, 128)))
        m = jnp.where(rows > j + 1, nxt, jnp.where(rows == j + 1, jnp.broadcast_to(r1, (K, 128)), m))
    diag = jnp.sum(jnp.where(rows == lanes, m, 0.0), axis=1, keepdims=True)
    linv = pltpu.roll(m, 128 - K, 1) * (1.0 / jnp.sqrt(diag))
    linv = linv[:, 0:K]
    for i in range(3):
        bas_ref[i] = jnp.dot(linv, img_in[i], preferred_element_type=F32, precision=HIGHEST)
        img_ref[i] = img_in[i]
    nm_ref[...] = nm_in[...]


def per_device(frames, mean_structure, atom_weight, subspace):
    x = jnp.transpose(frames, (1, 0, 2))
    s = jnp.transpose(subspace, (1, 0, 2))
    vm = pl.BlockSpec(memory_space=pltpu.VMEM)
    anyspec = pl.BlockSpec(memory_space=pl.ANY)
    dma = pltpu.SemaphoreType.DMA
    V = pltpu.VMEM
    scratch = [
        V((3, AL), F32), V((1, AL), F32), V((3, NF, AL), F32), V((3, K, AL), BF16), V((NB, 3, 2 * FP, BLK), BF16), V((NB, 3, FP, BLK), BF16),
        V((12, NF, 128), F32), V((NY, 8, 128), F32), V((NY, 8, 128), F32), V((2, K, 128), F32), V((K, 128), F32),
        V((NB * NC, 1, 128), F32), V((K, 128), BF16),
        V((NX * NC * NY, 8, 128), F32), V((NZ, 8, 128), F32),
        V((8, 2, 64, BLK), BF16), V((8, NX // 2, 2, 64, BLK), BF16),
        V((4, 80, BLK), BF16), V((4, NZ // 2, 80, BLK), BF16),
        V((NZ, 64, BLK), BF16), V((NZ, 64, BLK), BF16), V((2, 32, BLK), BF16), V((2, 32, BLK), BF16),
        V((NX, 48, BLK), BF16), V((NX, 48, BLK), BF16),
        V((NZ, 64, BLK), F32), V((2, 80, BLK), F32),
        V((4, 2, 64, BLK), F32), V((4, NZ // 2 - 1, 80, BLK), F32),
        dma, dma, dma((CHUNKS,)), dma,
        dma((NY - 1,)), dma((NY - 1,)), dma((NY - 1,)), dma((NY - 1,)),
        dma((NB * NC - 1,)), dma((NB * NC - 1,)),
        dma, dma, dma, dma,
        dma((NX * NC * NY - 1,)), dma((NX * NC * NY - 1,)), dma((NZ - 1,)), dma((NZ - 1,)),
        dma((8, NX // 2, 1)), dma((8, NX // 2, 1)), dma((4, NZ // 2, 2)), dma((4, NZ // 2, 2)),
        dma((NZ,)), dma((NZ,)), dma((2,)), dma((2,)), dma((NX,)), dma((NX,)),
    ]
    shapes = [(3, BLK), (3, K, BLK), (8, 128)]
    nm, img, gram = pl.pallas_call(
        kernel,
        out_shape=tuple(jax.ShapeDtypeStruct(d, F32) for d in shapes),
        in_specs=[anyspec] * 4,
        out_specs=(vm, vm, vm),
        scratch_shapes=scratch,
        compiler_params=pltpu.CompilerParams(
            collective_id=0, has_side_effects=True, vmem_limit_bytes=60 * 1024 * 1024
        ),
    )(x, mean_structure, atom_weight.reshape(1, AL), s)
    shapes = [(3, BLK), (3, K, BLK), (3, K, BLK)]
    nm, img, bas = pl.pallas_call(
        finish,
        out_shape=tuple(jax.ShapeDtypeStruct(d, F32) for d in shapes),
        in_specs=[vm, vm, vm],
        out_specs=(vm, vm, vm),
    )(nm, img, gram)
    return nm, jnp.transpose(img, (1, 0, 2)), jnp.transpose(bas, (1, 0, 2))


def solution(mesh):
    return jax.shard_map(
        per_device,
        mesh=mesh,
        in_specs=(P("frames", None, "atoms"), P(None, "atoms"), P("atoms"), P(None, None, "atoms")),
        out_specs=(
            P(None, ("atoms", "frames")),
            P(None, None, ("atoms", "frames")),
            P(None, None, ("atoms", "frames")),
        ),
        check_vma=False,
    )
```

```python
import jax
import jax.numpy as jnp
from jax import lax
from jax.experimental import pallas as pl
from jax.experimental.pallas import tpu as pltpu
from jax.sharding import PartitionSpec as P

ATOMS = 98304
FRAMES = 1536
NEWTON = 8
NX, NZ, NC, NY = 4, 8, 2, 4
NF = 24
FP = 32
K = 32
AL = ATOMS // NY
BLK = AL // (NX * NZ * NC)
NB = NX * NZ
CHUNKS = 8
CW = AL // CHUNKS
STEP = 1024
UNROLL = 16
VLHS = False
F32 = jnp.float32
BF16 = jnp.bfloat16
MESH = pl.DeviceIdType.MESH
HIGHEST = lax.Precision.HIGHEST
PARTS = ((3, 4), (5, 2), (6, 1), (7, 0))
NT = (((1,), (1,)), ((), ()))


def steps_of(n, half, direction):
    return n // 2 if (direction == 1) == (half == 0) else n // 2 - 1


def newton(m):
    norm = m[0] * m[0]
    for e in m[1:]:
        norm = norm + e * e
    inv = 1.0 / jnp.sqrt(norm)
    x = [e * inv for e in m]
    for _ in range(NEWTON):
        x00, x01, x02, x10, x11, x12, x20, x21, x22 = x
        cof = [
            x11 * x22 - x12 * x21,
            x12 * x20 - x10 * x22,
            x10 * x21 - x11 * x20,
            x02 * x21 - x01 * x22,
            x00 * x22 - x02 * x20,
            x01 * x20 - x00 * x21,
            x01 * x12 - x02 * x11,
            x02 * x10 - x00 * x12,
            x00 * x11 - x01 * x10,
        ]
        det = x00 * cof[0] + x01 * cof[1] + x02 * cof[2]
        r = 1.0 / det
        x = [0.5 * (a + c * r) for a, c in zip(x, cof)]
    return x


def kernel(
    x_hbm, ms_hbm, w_hbm, s_hbm, nm_ref, img_ref, g_ref,
    ms_ref, w_ref, xv, sv, dall, dsend, rot, ex1, ex2, pp, gsq, pba, cpt, gx, gz,
    a1s, a1r, b1s, b1r, a2s, a2r, h4s, h4r, b2s, b2r, acca, accb, taf, tbf,
    msem, wsem, xsem, ssem, y1s, y1r, y2s, y2r, px_s, px_r, pp_s, pp_r, dx_s, dx_r,
    gx_s, gx_r, gz_s, gz_r, a1ss, a1rs, b1ss, b1rs, a2ss, a2rs, h4ss, h4rs, b2ss, b2rs,
):
    y = lax.axis_index("atoms")
    n = lax.axis_index("frames")
    px = n // (NZ * NC)
    pz = (n // NC) % NZ
    pc = n % NC

    def dev(dx=0, dz=0, dc=0, dy=0):
        tx = (px + (dx + NX)) % NX
        tz = (pz + (dz + NZ)) % NZ
        tc = (pc + dc) % NC
        return ((y + dy) % NY, (tx * NZ + tz) * NC + tc)

    def hops(o):
        return sum(min(k, size - k) for k, size in zip(o, (NX, NY, NZ)))

    def peers(nx, ny, nz, nc):
        offsets = [
            (a, b, c, e) for a in range(nx) for b in range(ny) for c in range(nz) for e in range(nc) if a + b + c + e
        ]
        offsets.sort(key=lambda o: -hops(o))
        return [dev(dx=a, dy=b, dz=c, dc=e) for a, b, c, e in offsets]

    y_peers = peers(1, NY, 1, 1)
    f_peers = peers(NX, 1, NZ, NC)
    p_peers = peers(NX, NY, 1, NC)
    z_far = peers(1, 1, NZ, 1)
    greet = f_peers + [dev(dx=a, dy=b, dc=e) for a in range(NX) for b in range(1, NY) for e in range(NC)]
    z_peers = [dev(dz=j) for j in range(1, NZ)]
    partner = dev(dc=1)

    mload = pltpu.make_async_copy(ms_hbm, ms_ref, msem)
    wload = pltpu.make_async_copy(w_hbm, w_ref, wsem)
    wload.start()
    mload.start()
    loads = []
    for q in range(CHUNKS):
        cols = pl.ds(q * CW, CW)
        cp = pltpu.make_async_copy(x_hbm.at[:, :, cols], xv.at[:, :, cols], xsem.at[q])
        loads.append(cp)
    for cp in loads[:2]:
        cp.start()
    sload = pltpu.make_async_copy(s_hbm, sv, ssem)

    barrier = pltpu.get_barrier_semaphore()
    for peer in greet:
        pl.semaphore_signal(barrier, inc=1, device_id=peer, device_id_type=MESH)

    def remote(src, dst, ssm, rsm, peer):
        return pltpu.make_async_remote_copy(
            src_ref=src, dst_ref=dst, send_sem=ssm, recv_sem=rsm, device_id=peer, device_id_type=MESH
        )

    pending = []

    def exchange(buf, peers, ssm, rsm):
        copies = []
        for j, peer in enumerate(peers):
            copies.append(remote(buf.at[0], buf.at[j + 1], ssm.at[j], rsm.at[j], peer))
        for c in copies:
            c.start()
        for c in copies:
            c.wait_recv()
        pending.extend(copies)

    lane = lax.broadcasted_iota(jnp.int32, (NF, 128), 1)

    wload.wait()
    mload.wait()
    for cp in loads[2:]:
        cp.start()
    lc = jnp.sum(ms_ref[:, 0:2048], axis=1, keepdims=True) * (1.0 / 2048)

    def sums_body(q, acc):
        acc = list(acc)
        tw, tm = acc[12:]
        cols = pl.ds(pl.multiple_of(q * STEP, STEP), STEP)
        wv = w_ref[:, cols]
        wm = (ms_ref[:, cols] - lc) * wv
        for t in range(STEP // 128):
            lo = t * 128
            tw = tw + wv[:, lo : lo + 128]
            tm = tm + wm[:, lo : lo + 128]
            sub = pl.ds(pl.multiple_of(q * STEP + lo, 128), 128)
            wt = jnp.broadcast_to(wv[:, lo : lo + 128], (NF, 128))
            mt = [jnp.broadcast_to(wm[i : i + 1, lo : lo + 128], (NF, 128)) for i in range(3)]
            for j in range(3):
                xj = xv[j, :, sub]
                acc[j] = acc[j] + xj * wt
                for i in range(3):
                    acc[3 + i * 3 + j] = acc[3 + i * 3 + j] + xj * mt[i]
        acc[12:] = [tw, tm]
        return tuple(acc)

    acc = tuple(jnp.zeros((NF, 128), F32) for _ in range(12))
    acc += (jnp.zeros((1, 128), F32), jnp.zeros((3, 128), F32))
    per = CW // STEP
    for q in range(CHUNKS):
        if q == CHUNKS - 1:
            sload.start()
        loads[q].wait()
        acc = lax.fori_loop(q * per, (q + 1) * per, sums_body, acc)
    tw = jnp.sum(acc[12], axis=1, keepdims=True)
    tm = jnp.sum(acc[13], axis=1, keepdims=True) + lc * tw
    sums = [jnp.broadcast_to(jnp.sum(a, axis=1, keepdims=True), (NF, 128)) for a in acc[:12]]
    wide = [jnp.broadcast_to(lc[i : i + 1], (NF, 128)) for i in range(3)]
    wide_m = [jnp.broadcast_to(tm[i : i + 1], (NF, 128)) for i in range(3)]
    tile = jnp.broadcast_to(tw, (NF, 128))
    for i in range(3):
        for j in range(3):
            e = 3 * i + j
            tile = jnp.where(lane == e, sums[3 + e], tile)
            tile = jnp.where(lane == 9 + e, sums[j], tile)
            tile = jnp.where(lane == 18 + e, wide[i], tile)
            tile = jnp.where(lane == 27 + e, wide_m[i], tile)
    tile = jnp.where(lane < 42, tile, 0.0)
    ex1[0] = tile[0:8] + pltpu.roll(tile[8:16], 42, 1) + pltpu.roll(tile[16:24], 84, 1)
    pl.semaphore_wait(barrier, len(greet))
    exchange(ex1, y_peers, y1s, y1r)

    slots = []
    for j in range(NY):
        v = ex1[j]
        slots.append(jnp.concatenate([v, pltpu.roll(v, 128 - 42, 1), pltpu.roll(v, 128 - 84, 1)], axis=0))
    tsum = slots[0] + slots[1] + slots[2] + slots[3]
    inv_total = 1.0 / jnp.broadcast_to(tsum[:, 36:37], (NF, 128))
    tsum = tsum * inv_total
    mrep = pltpu.roll(tsum, 128 - 27, 1)
    packed = None
    for p in slots:
        t = p + (pltpu.roll(p, 128 - 18, 1) - mrep) * pltpu.roll(p, 128 - 9, 1)
        packed = t if packed is None else packed + t
    packed = packed * inv_total
    r = newton([jnp.broadcast_to(packed[:, q : q + 1], (NF, 128)) for q in range(9)])
    fc = [jnp.broadcast_to(tsum[:, 9 + j : 10 + j], (NF, 128)) for j in range(3)]
    mc = [jnp.broadcast_to(tsum[:, 27 + 3 * i : 28 + 3 * i], (NF, 128)) for i in range(3)]
    for q in range(9):
        rot[q] = r[q]
    for i in range(3):
        off = r[3 * i] * fc[0] + r[3 * i + 1] * fc[1] + r[3 * i + 2] * fc[2]
        rot[9 + i] = mc[i] - off

    sload.wait()

    def move_body(own):
        def body(g, acc):
            core = pc if own else 1 - pc
            for i in range(3):
                vs, ss = [], []
                for u in range(UNROLL):
                    b = g * UNROLL + u
                    base = (b * NC + core) * BLK
                    pieces = []
                    for t in range(BLK // 128):
                        sub = pl.ds(pl.multiple_of(base + t * 128, 128), 128)
                        v = rot[3 * i] * xv[0, :, sub] + rot[3 * i + 1] * xv[1, :, sub] + rot[3 * i + 2] * xv[2, :, sub]
                        v = v + rot[9 + i] - jnp.broadcast_to(ms_ref[i : i + 1, sub], (NF, 128))
                        pieces.append(v)
                    v = jnp.concatenate(pieces, axis=1)
                    v = jnp.concatenate([v, jnp.zeros((FP - NF, BLK), F32)], axis=0).astype(BF16)
                    if own:
                        dall[b, i, 0:FP, :] = v
                    else:
                        dsend[b, i] = v
                    vs.append(v)
                    ss.append(sv[i, :, pl.ds(pl.multiple_of(base, 128), BLK)])
                vs = jnp.concatenate(vs, axis=1)
                ss = jnp.concatenate(ss, axis=1)
                if VLHS:
                    acc = acc + lax.dot_general(vs, ss, NT, preferred_element_type=F32)
                else:
                    acc = acc + lax.dot_general(ss, vs, NT, preferred_element_type=F32)
            return acc

        return body

    pacc = lax.fori_loop(0, NB // UNROLL, move_body(False), jnp.zeros((K, FP), F32))
    dcopy = remote(dsend, dall.at[:, :, FP : 2 * FP, :], dx_s, dx_r, partner)
    dcopy.start()
    pacc = lax.fori_loop(0, NB // UNROLL, move_body(True), pacc)
    if VLHS:
        pacc = pacc.T

    rows = lax.broadcasted_iota(jnp.int32, (K, 128), 0)
    lanes = lax.broadcasted_iota(jnp.int32, (K, 128), 1)
    gsq[...] = jnp.zeros((K, 128), F32)
    gsq[:, 0:FP] = pacc
    v = gsq[0:8, :]
    for q in range(1, 4):
        v = v + pltpu.roll(gsq[8 * q : 8 * q + 8, :], 32 * q, 1)
    ex2[0] = v
    exchange(ex2, y_peers, y2s, y2r)
    v = ex2[0] + ex2[1] + ex2[2] + ex2[3]
    ptot = jnp.concatenate([v] + [pltpu.roll(v, 128 - 32 * q, 1) for q in range(1, 4)], axis=0)
    ptot = jnp.where(lanes < FP, ptot, 0.0)
    pp[0] = ptot
    pcopy = remote(pp.at[0], pp.at[1], pp_s, pp_r, partner)
    pcopy.start()
    col = jnp.broadcast_to(jnp.sum(ptot, axis=1, keepdims=True), (K, 128))
    row = jnp.sum(jnp.where(rows == lanes, col, 0.0), axis=0, keepdims=True)
    pba[0] = row
    exchange(pba, f_peers, px_s, px_r)
    row = jnp.broadcast_to(jnp.sum(pba[...], axis=0), (K, 128))
    pbar = jnp.sum(jnp.where(rows == lanes, row, 0.0), axis=1, keepdims=True) / FRAMES
    pcopy.wait_recv()
    other = pltpu.roll(pp[1], FP, 1)
    both = jnp.where(lanes < FP, ptot, other) - pbar
    cpt[...] = both.astype(BF16)
    dcopy.wait_recv()

    erow = lax.broadcasted_iota(jnp.int32, (16, 2 * FP), 0)
    ones = [jnp.where(erow == i, 1.0, 0.0).astype(BF16) for i in range(6)]
    coef = cpt[:, 0 : 2 * FP]
    coef2 = [jnp.concatenate([coef, ones[3 * q + 2]], axis=0) for q in range(2)]

    def mm(lhs, rhs):
        return jnp.dot(lhs, rhs, preferred_element_type=F32)

    def zblk(g, q):
        return (pz + PARTS[g][q]) % NZ

    def term_a(dest, g, emit):
        for q in range(2):
            blk = dest * NZ + zblk(g, q)
            for i in range(2):
                emit(q, i, mm(coef, dall[blk, i]))

    def term_b(dest, h, ref):
        tail = None
        for q in range(2):
            blk = (h * (NX // 2) + q) * NZ + dest
            t = mm(coef2[q], dall[blk, 2])
            ref[32 * q : 32 * q + 32, :] = t[0:32].astype(ref.dtype)
            t = t[32:48] + (mm(ones[3 * q], dall[blk, 0]) + mm(ones[3 * q + 1], dall[blk, 1]))
            tail = t if tail is None else tail + t
        ref[64:80, :] = tail.astype(ref.dtype)

    def rowslice(i):
        return slice(32 * i, 32 * i + 32)

    def store(ref, rows_of):
        def emit(q, i, t):
            ref[q, rows_of(i), :] = t.astype(ref.dtype)

        return emit

    class Stage:
        def __init__(self, length, pos, parts, sbuf, rbuf, ssm, rsm, fill, peer_of, subs):
            self.length, self.pos, self.sbuf, self.rbuf = length, pos, sbuf, rbuf
            self.ssm, self.rsm, self.fill, self.peer_of, self.subs = ssm, rsm, fill, peer_of, subs
            self.streams = tuple((h, d) for h in range(parts) for d in (1, -1))
            self.copies = {}
            self.filled = set()

        def steps(self, st):
            h, d = self.streams[st]
            return steps_of(self.length, h % 2, d)

        def dest(self, st, s):
            h, d = self.streams[st]
            return (self.pos + (d * (self.steps(st) - s) + self.length)) % self.length

        def prepare(self, st):
            self.fill(self.sbuf.at[st], st, 0, None)
            self.filled.add(st)

        def send(self, st, s):
            h, d = self.streams[st]
            if s >= self.steps(st):
                return
            if s == 0:
                src = self.sbuf.at[st]
                if st not in self.filled:
                    self.prepare(st)
            else:
                src = self.rbuf.at[st, s - 1]
            for k, sub in enumerate(self.subs):
                if s:
                    self.copies[st, s - 1, k].wait_recv()
                    self.fill(src.at[sub], st, s, sub)
                c = remote(
                    src.at[sub], self.rbuf.at[st, s].at[sub], self.ssm.at[st, s, k], self.rsm.at[st, s, k],
                    self.peer_of(d),
                )
                c.start()
                pending.append(c)
                self.copies[st, s, k] = c

        def finals(self, h):
            out = []
            for st, (hh, d) in enumerate(self.streams):
                if hh == h:
                    s = self.steps(st) - 1
                    for k in range(len(self.subs)):
                        self.copies[st, s, k].wait_recv()
                    out.append(self.rbuf.at[st, s])
            return out

    def fill_a1(ref, st, s, sub):
        g = st // 2
        if s == 0:
            term_a(sa1.dest(st, 0), g, store(ref, rowslice))
        else:
            ref[...] = (taf[g] + ref[...].astype(F32)).astype(BF16)

    def fill_b1(ref, st, s, sub):
        if s == 0:
            term_b(sb1.dest(st, 0), st // 2, ref)
        else:
            ref[...] = (tbf[st, s - 1, sub] + ref[...].astype(F32)).astype(BF16)

    x_dir = {1: dev(dx=1), -1: dev(dx=-1)}
    z_dir = {1: dev(dz=1), -1: dev(dz=-1)}
    sa1 = Stage(NX, px, 4, a1s, a1r, a1ss, a1rs, fill_a1, x_dir.get, (slice(0, 2),))
    sb1 = Stage(NZ, pz, 2, b1s, b1r, b1ss, b1rs, fill_b1, z_dir.get, (slice(0, 32), slice(32, 80)))

    order = (0, 3, 2, 1)
    for st in order:
        sa1.send(st, 0)
        sb1.send(st, 0)

    def terms_b(s):
        for st in order:
            if s < sb1.steps(st):
                term_b(sb1.dest(st, s), st // 2, tbf.at[st, s - 1])

    def terms_a(st):
        term_a(sa1.dest(st, 1), st // 2, store(taf.at[st // 2], rowslice))

    terms_a(0)
    terms_a(3)
    terms_b(1)
    for st in (4, 7, 6, 5):
        sa1.prepare(st)
    for st in (0, 3):
        sb1.send(st, 1)
        sa1.send(st, 1)
    for st in (4, 7, 6, 5):
        sa1.send(st, 0)
    for st in (2, 1):
        sb1.send(st, 1)
    terms_b(2)
    terms_b(3)
    terms_a(4)
    terms_a(7)

    def own_a(g):
        def emit(q, i, t):
            acca[zblk(g, q), rowslice(i), :] = t

        term_a(px, g, emit)

    def fin_a(g):
        f0, f1 = sa1.finals(g)
        for q in range(2):
            z = zblk(g, q)
            acca[z] = acca[z] + (f0[q].astype(F32) + f1[q].astype(F32))

    own_a(0)
    own_a(1)
    for st in order:
        sb1.send(st, 2)

    second = {}

    def straight(key, src, dst, ssm, rsm, peer):
        c = remote(src, dst, ssm, rsm, peer)
        c.start()
        pending.append(c)
        second[key] = c

    def send_z(r, merged=None):
        t = acca[(pz + r) % NZ]
        if merged is None:
            a2s[r] = t.astype(BF16)
        else:
            half = rowslice(merged)
            second["h", merged].wait_recv()
            a2s[r] = t.astype(BF16)
            a2s[r, half, :] = (acca[(pz + r) % NZ, half, :] + h4r[merged].astype(F32)).astype(BF16)
        straight(("z", r), a2s.at[r], a2r.at[r], a2ss.at[r], a2rs.at[r], z_peers[r - 1])

    fin_a(0)
    fin_a(1)
    for h, d in ((0, 1), (1, -1)):
        h4s[h] = acca[(pz + 4) % NZ, rowslice(h), :].astype(BF16)
        straight(("h", h), h4s.at[h], h4r.at[h], h4ss.at[h], h4rs.at[h], z_dir[d])
    own_a(2)
    own_a(3)
    for h in (0, 1):
        term_b(pz, h, accb.at[h])
    sa1.send(4, 1)
    sa1.send(7, 1)
    for st in order:
        sb1.send(st, 3)
    send_z(3, 0)
    send_z(5, 1)
    send_z(2)
    fin_a(2)
    fin_a(3)
    for r in (6, 1, 7):
        send_z(r)
    for h in (0, 1):
        f0, f1 = sb1.finals(h)
        accb[h] = accb[h] + (f0[...].astype(F32) + f1[...].astype(F32))

    def own_b(e):
        return accb[e // 2, pl.ds(pl.multiple_of(e % 2 * 32, 32), 32), :]

    for d in (2, 1, 3):
        e = (px + d) % NX
        b2s[d, 0:32, :] = own_b(e).astype(BF16)
        b2s[d, 32:48, :] = accb[e // 2, 64:80, :].astype(BF16)
        straight(("x", d), b2s.at[d], b2r.at[d], b2ss.at[d], b2rs.at[d], dev(dx=d))

    inv_f = 1.0 / FRAMES
    whole = acca[pz]
    for r in (2, 3, 5, 6, 1, 7):
        second["z", r].wait_recv()
        whole = whole + a2r[r].astype(F32)
    whole = whole * inv_f
    img2 = own_b(px)
    shift = accb[px // 2, 64:80, :]
    for d in (2, 1, 3):
        second["x", d].wait_recv()
        img2 = img2 + b2r[d, 0:32, :].astype(F32)
        shift = shift + b2r[d, 32:48, :].astype(F32)
    img2 = img2 * inv_f
    shift = jnp.where(px % 2 == 0, shift[0:3], shift[3:6])
    own = pl.ds(pl.multiple_of(n * BLK, 128), BLK)
    nm_ref[...] = ms_ref[:, own] + shift * inv_f
    imgs = [whole[0:32], whole[32:64]]
    imgs.append(img2)
    g = None
    for i in range(3):
        img_ref[i] = imgs[i]
        t = lax.dot_general(imgs[i], imgs[i], NT, preferred_element_type=F32, precision=HIGHEST)
        g = t if g is None else g + t
    gsq[...] = jnp.zeros((K, 128), F32)
    gsq[:, 0:K] = g
    v = gsq[0:8, :]
    for q in range(1, 4):
        v = v + pltpu.roll(gsq[8 * q : 8 * q + 8, :], 32 * q, 1)
    gx[0] = v
    exchange(gx, p_peers, gx_s, gx_r)
    gz[0] = jnp.sum(gx[...], axis=0)
    exchange(gz, z_far, gz_s, gz_r)
    v = gz[0]
    for j in range(1, NZ):
        v = v + gz[j]
    g_ref[...] = v / (3 * ATOMS)

    for c in pending + [dcopy, pcopy]:
        c.wait_send()


def finish(nm_in, img_in, g_ref, nm_ref, img_ref, bas_ref):
    rows = lax.broadcasted_iota(jnp.int32, (K, 128), 0)
    lanes = lax.broadcasted_iota(jnp.int32, (K, 128), 1)
    v = g_ref[...]
    m = jnp.concatenate([v] + [pltpu.roll(v, 128 - 32 * q, 1) for q in range(1, 4)], axis=0)
    m = jnp.where(lanes < K, m, jnp.where(lanes - K == rows, 1.0, 0.0))
    for j in range(0, K, 2):
        r0 = m[j : j + 1, :]
        r1 = m[j + 1 : j + 2, :]
        c0 = jnp.broadcast_to(m[:, j : j + 1], (K, 128))
        c1 = jnp.broadcast_to(m[:, j + 1 : j + 2], (K, 128))
        ia = 1.0 / c0[j : j + 1, :]
        ratio = c0[j + 1 : j + 2, :] * ia
        r1 = r1 - ratio * r0
        u1 = r1 * (1.0 / (c1[j + 1 : j + 2, :] - ratio * c1[j : j + 1, :]))
        u0 = (r0 - c1[j : j + 1, :] * u1) * ia
        nxt = m - (c0 * jnp.broadcast_to(u0, (K, 128)) + c1 * jnp.broadcast_to(u1, (K, 128)))
        m = jnp.where(rows > j + 1, nxt, jnp.where(rows == j + 1, jnp.broadcast_to(r1, (K, 128)), m))
    diag = jnp.sum(jnp.where(rows == lanes, m, 0.0), axis=1, keepdims=True)
    linv = pltpu.roll(m, 128 - K, 1) * (1.0 / jnp.sqrt(diag))
    linv = linv[:, 0:K]
    for i in range(3):
        bas_ref[i] = jnp.dot(linv, img_in[i], preferred_element_type=F32, precision=HIGHEST)
        img_ref[i] = img_in[i]
    nm_ref[...] = nm_in[...]


def per_device(frames, mean_structure, atom_weight, subspace):
    x = jnp.transpose(frames, (1, 0, 2))
    s = jnp.transpose(subspace, (1, 0, 2))
    vm = pl.BlockSpec(memory_space=pltpu.VMEM)
    anyspec = pl.BlockSpec(memory_space=pl.ANY)
    dma = pltpu.SemaphoreType.DMA
    V = pltpu.VMEM
    scratch = [
        V((3, AL), F32), V((1, AL), F32), V((3, NF, AL), F32), V((3, K, AL), BF16), V((NB, 3, 2 * FP, BLK), BF16), V((NB, 3, FP, BLK), BF16),
        V((12, NF, 128), F32), V((NY, 8, 128), F32), V((NY, 8, 128), F32), V((2, K, 128), F32), V((K, 128), F32),
        V((NB * NC, 1, 128), F32), V((K, 128), BF16),
        V((NX * NC * NY, 8, 128), F32), V((NZ, 8, 128), F32),
        V((8, 2, 64, BLK), BF16), V((8, NX // 2, 2, 64, BLK), BF16),
        V((4, 80, BLK), BF16), V((4, NZ // 2, 80, BLK), BF16),
        V((NZ, 64, BLK), BF16), V((NZ, 64, BLK), BF16), V((2, 32, BLK), BF16), V((2, 32, BLK), BF16),
        V((NX, 48, BLK), BF16), V((NX, 48, BLK), BF16),
        V((NZ, 64, BLK), F32), V((2, 80, BLK), F32),
        V((4, 2, 64, BLK), F32), V((4, NZ // 2 - 1, 80, BLK), F32),
        dma, dma, dma((CHUNKS,)), dma,
        dma((NY - 1,)), dma((NY - 1,)), dma((NY - 1,)), dma((NY - 1,)),
        dma((NB * NC - 1,)), dma((NB * NC - 1,)),
        dma, dma, dma, dma,
        dma((NX * NC * NY - 1,)), dma((NX * NC * NY - 1,)), dma((NZ - 1,)), dma((NZ - 1,)),
        dma((8, NX // 2, 1)), dma((8, NX // 2, 1)), dma((4, NZ // 2, 2)), dma((4, NZ // 2, 2)),
        dma((NZ,)), dma((NZ,)), dma((2,)), dma((2,)), dma((NX,)), dma((NX,)),
    ]
    shapes = [(3, BLK), (3, K, BLK), (8, 128)]
    nm, img, gram = pl.pallas_call(
        kernel,
        out_shape=tuple(jax.ShapeDtypeStruct(d, F32) for d in shapes),
        in_specs=[anyspec] * 4,
        out_specs=(vm, vm, vm),
        scratch_shapes=scratch,
        compiler_params=pltpu.CompilerParams(
            collective_id=0, has_side_effects=True, vmem_limit_bytes=60 * 1024 * 1024
        ),
    )(x, mean_structure, atom_weight.reshape(1, AL), s)
    shapes = [(3, BLK), (3, K, BLK), (3, K, BLK)]
    nm, img, bas = pl.pallas_call(
        finish,
        out_shape=tuple(jax.ShapeDtypeStruct(d, F32) for d in shapes),
        in_specs=[vm, vm, vm],
        out_specs=(vm, vm, vm),
    )(nm, img, gram)
    return nm, jnp.transpose(img, (1, 0, 2)), jnp.transpose(bas, (1, 0, 2))


def solution(mesh):
    return jax.shard_map(
        per_device,
        mesh=mesh,
        in_specs=(P("frames", None, "atoms"), P(None, "atoms"), P("atoms"), P(None, None, "atoms")),
        out_specs=(
            P(None, ("atoms", "frames")),
            P(None, None, ("atoms", "frames")),
            P(None, None, ("atoms", "frames")),
        ),
        check_vma=False,
    )
```
